32 devices in a mesh: gx: 4 (over z), gy: 8 (over y, x, core).
Axes of the slice: x: 2, y: 2, z: 4, core: 2. Of those that a mesh axis runs over, the one named last changes fastest.
Arguments:
- tokens: bfloat16 [512, 3584], P(('gx', 'gy')), may hold values from -6 to 6
- expert_ids: int32 [512, 8], P(('gx', 'gy')), may hold values from 0 to 31, all different within a row; in each aligned block of 16 rows (0 to 15, 16 to 31, ...) at most 6 rows name the same one
- backup_ids: int32 [512, 8], P(('gx', 'gy')), may hold values from 0 to 31, all different within a row; in each aligned block of 16 rows (0 to 15, 16 to 31, ...) at most 6 rows name the same one
- scores: float32 [512, 8], P(('gx', 'gy')), may hold values from 0.05 to 1
- gate_weight: bfloat16 [32, 3584, 1024], P(('gx', 'gy')), may hold values from -0.09375 to 0.09375
- up_weight: bfloat16 [32, 3584, 1024], P(('gx', 'gy')), may hold values from -0.09375 to 0.09375
- down_weight: bfloat16 [32, 1024, 3584], P(('gx', 'gy')), may hold values from -0.1875 to 0.1875
Outputs:
- mixed: bfloat16 [512, 3584], P(('gx', 'gy'))
The draws below stay inside these ranges and needn't reach their ends.
Inputs may be any that keep to these rules, and one draw needn't show every extreme that they name: `expert_ids`: among the rows of one device no expert number is named more than 6 times. `backup_ids`: among the rows of one device no expert number is named more than 6 times.
All inputs are finite; a program needn't handle non-finite values.
Results may differ from the reference program's by a relative error of at most 0.0058.
Values may be sent and summed in bfloat16 or wider, within the bound.
A program may use at most 128 MiB of HBM per device.

```python
import math
import jax
import jax.numpy as jnp
import numpy as np
from jax import lax

D = 3584
FF = 1024
TOP = 8
TOK_DEV = 16
EXPERTS = 32
TOKENS = 512
MOST = 6
CAP = 128
QUOTA = 1
SPARE = 32


def level_of(stream_key, shape, cuts, low, top_value):
    factor_of, own = 1.0, jax.random.fold_in(stream_key, 6)
    for axis_at, parts in cuts:
        heights = jnp.exp(jax.random.uniform(jax.random.fold_in(own, axis_at), (parts,), jnp.float32, low / len(cuts), top_value / len(cuts)))
        factor_of = factor_of * jnp.repeat(heights, shape[axis_at] // parts).reshape([-1 if axis == axis_at else 1 for axis in range(len(shape))])
    return factor_of


def deal_out(own_key, own, number, rows, count, top, most, lean):
    ranking = jax.random.permutation(own_key, count)
    crowded, common = load_shares(count, rows * top, most, lean, True), load_shares(count, rows * top, most, lean, False)
    places = jnp.arange(count)

    def named(tallies, turn):
        used = int((tallies > 0).sum())
        fixed = max(1, used // 4)
        moved = fixed + (places - fixed + turn * (used - fixed)) % max(1, count - fixed)
        return jnp.zeros((count,), jnp.int32).at[ranking[jnp.where(places < fixed, places, moved)]].set(jnp.asarray(tallies, jnp.int32))

    tallies = jnp.where(number % 4 == 0, named(crowded, number // 4), named(common, number - number // 4 - 1))
    mixed = jax.random.permutation(jax.random.fold_in(own, 3), count)
    donor, taker = mixed[0:count // 2 * 2:2], mixed[1:count // 2 * 2:2]
    room = jnp.minimum(tallies[donor] - 1, most - tallies[taker]) // 2
    room = jnp.where((donor == ranking[0]) | (taker == ranking[0]) | (tallies[taker] == 0), 0, jnp.maximum(room, 0))
    moved = jax.random.randint(jax.random.fold_in(own, 4), (count // 2,), 0, 1 << 20) % (room + 1)
    tallies = tallies.at[donor].add(-moved).at[taker].add(moved)
    labels = jnp.searchsorted(jnp.cumsum(tallies), jnp.arange(rows * top), side="right").astype(jnp.int32)
    table = labels.reshape(top, rows).T
    table = table[jax.random.permutation(jax.random.fold_in(own, 1), rows)]
    turn = jax.random.randint(jax.random.fold_in(own, 2), (rows, 1), 0, top)
    return jnp.take_along_axis(table, (jnp.arange(top)[None, :] + turn) % top, axis=1)


def load_shares(count, total, reach, skew, full):
    weights = [(1 << 20) // math.isqrt(rank ** skew) + 1 for rank in range(1, count + 1)]
    largest = reach if full else min(reach, max(-(-total // count), total * weights[0] // sum(weights)))
    least = 1 if total - largest >= count - 1 else 0
    counts, surplus = [largest] + [least] * (count - 1), total - largest - least * (count - 1)
    while surplus > 0:
        candidates = [i for i in range(1, count) if counts[i] < largest] or [i for i in range(1, count) if counts[i] < reach]
        whole, left = sum([weights[i] for i in candidates]), surplus
        for i in candidates:
            more = min(reach - counts[i], max(1, left * weights[i] // whole), surplus)
            counts[i] = counts[i] + more
            surplus = surplus - more
    return np.array(counts)


def bell_draw(key, dims, deviation, most, shards=(), held_as=jnp.bfloat16):
    result = jax.random.normal(key, dims, jnp.float32) * deviation
    if len(shards) > 0:
        result = level_of(key, dims, shards, -0.22, 0.18) * result
    return jnp.clip(result, min=-most, max=most).astype(held_as)


def setup_inputs(seed: int = 0) -> dict:
    key_list = jax.random.split(jax.random.key(seed), 8)
    tokens = bell_draw(key_list[0], (TOKENS, D), 1.0, 6.0, ((0, 32),))
    expert_ids_keys = jax.random.split(jax.random.fold_in(key_list[1], 1), TOKENS // TOK_DEV)
    expert_ids_turns = jax.random.permutation(jax.random.fold_in(key_list[1], 3), TOKENS // TOK_DEV)
    expert_ids = jax.vmap(lambda own, number: deal_out(jax.random.fold_in(key_list[1], 2), own, number, TOK_DEV, EXPERTS, TOP, MOST, 2))(expert_ids_keys, expert_ids_turns).reshape((TOKENS, TOP))
    backup_ids_keys = jax.random.split(jax.random.fold_in(key_list[2], 1), TOKENS // TOK_DEV)
    backup_ids_turns = jax.random.permutation(jax.random.fold_in(key_list[2], 3), TOKENS // TOK_DEV)
    backup_ids = jax.vmap(lambda own, number: deal_out(jax.random.fold_in(key_list[2], 2), own, number, TOK_DEV, EXPERTS, TOP, MOST, 0))(backup_ids_keys, backup_ids_turns).reshape((TOKENS, TOP))
    scores = jnp.clip(jnp.exp(math.log(1.0) - 2.9957323 * jax.random.uniform(key_list[3], (TOKENS, TOP), jnp.float32) ** level_of(key_list[3], (TOKENS, TOP), ((0, 32),), -0.2, 0.2)), 0.05, 1.0)
    gate_weight = bell_draw(key_list[4], (EXPERTS, D, FF), D ** -0.5, 0.09375, ((0, 32),))
    up_weight = bell_draw(key_list[5], (EXPERTS, D, FF), D ** -0.5, 0.09375, ((0, 32),))
    down_weight = bell_draw(key_list[6], (EXPERTS, FF, D), FF ** -0.5, 0.1875, ((0, 32),))
    return dict(tokens=tokens, expert_ids=expert_ids, backup_ids=backup_ids, scores=scores, gate_weight=gate_weight, up_weight=up_weight, down_weight=down_weight)


def ranks_in_order(numbers, active):
    table = ((numbers[:, None] == jnp.arange(EXPERTS, dtype=jnp.int32)[None, :]) & active[:, None]).astype(jnp.int32)
    before = jnp.cumsum(table, axis=0) - table
    return jnp.sum(before * table, axis=1).astype(jnp.int32)


def reference(tokens, expert_ids, backup_ids, scores, gate_weight, up_weight, down_weight):
    choices = TOKENS * TOP
    per_source = TOK_DEV * TOP
    slots = CAP + SPARE
    first_flat = expert_ids.reshape(-1).astype(jnp.int32)
    backup_flat = backup_ids.reshape(-1).astype(jnp.int32)
    first_rank = ranks_in_order(first_flat, jnp.ones((choices,), dtype=bool))
    kept = first_rank < CAP
    spilled = jnp.logical_not(kept)
    spill_rank = jax.vmap(ranks_in_order)(backup_flat.reshape(EXPERTS, per_source),
                                          spilled.reshape(EXPERTS, per_source)).reshape(-1).astype(jnp.int32)
    spare_ok = spilled & (spill_rank < QUOTA)
    source_device = (jnp.arange(choices, dtype=jnp.int32) // per_source).astype(jnp.int32)
    outside = EXPERTS * slots
    target = jnp.where(kept, first_flat * slots + first_rank,
                       jnp.where(spare_ok, backup_flat * slots + CAP + source_device * QUOTA + spill_rank,
                                 outside)).astype(jnp.int32)
    sources = jnp.full((outside,), -1, dtype=jnp.int32)
    sources = sources.at[target].set(jnp.arange(choices, dtype=jnp.int32), mode="drop").reshape(EXPERTS, slots)

    def expert_block(inputs):
        source_list, w_gate, w_up, w_down = inputs
        token_index = (jnp.maximum(source_list, 0) // TOP).astype(jnp.int32)
        rows = jnp.where((source_list >= 0)[:, None], tokens[token_index], jnp.zeros((), jnp.bfloat16))
        gate = jnp.dot(rows, w_gate, preferred_element_type=jnp.float32)
        upward = jnp.dot(rows, w_up, preferred_element_type=jnp.float32)
        hidden = (jax.nn.silu(gate) * upward).astype(jnp.bfloat16)
        return jnp.dot(hidden, w_down, preferred_element_type=jnp.float32).astype(jnp.bfloat16)

    outputs = lax.map(expert_block, (sources, gate_weight, up_weight, down_weight))
    flat_out = outputs.reshape(outside, D)
    picked = jnp.take(flat_out, jnp.minimum(target, outside - 1), axis=0)
    valid = (kept | spare_ok).reshape(TOKENS, TOP)
    route_weights = scores / jnp.sum(scores, axis=1, keepdims=True)
    weights = jnp.where(valid, route_weights, jnp.zeros((), jnp.float32))
    mixed = jnp.sum(weights[:, :, None] * picked.reshape(TOKENS, TOP, D).astype(jnp.float32), axis=1)
    return mixed.astype(jnp.bfloat16)
```

```python
import functools
import jax
import jax.numpy as jnp
from jax import lax
from jax.experimental import pallas as pl
from jax.experimental.pallas import tpu as pltpu
from jax.sharding import PartitionSpec as P


def earlier_total(table):
    row = lax.broadcasted_iota(jnp.int32, (table.shape[0],) * 2, 0)
    col = lax.broadcasted_iota(jnp.int32, (table.shape[0],) * 2, 1)
    lower = (col < row).astype(jnp.bfloat16)
    total = jnp.dot(lower, table.astype(jnp.bfloat16), preferred_element_type=jnp.float32)
    return total.astype(jnp.int32)


def ranks_within(numbers, active, expert_count):
    table = (
        (numbers[:, None] == jnp.arange(expert_count, dtype=jnp.int32)[None, :]) & active[:, None]
    ).astype(jnp.int32)
    within = jnp.sum(earlier_total(table) * table, axis=1)
    return (within, table)


def pack_rows(tokens, destination, active, slot_total, top_count):
    pick_number = jnp.arange(destination.shape[0], dtype=jnp.int32)
    match_grid = (
        destination[None, :] == jnp.arange(slot_total, dtype=jnp.int32)[:, None]
    ) & active[None, :]
    source = jnp.sum(jnp.where(match_grid, pick_number[None, :] + 1, 0), axis=1) - 1
    picked_rows = jnp.take(tokens, jnp.maximum(source, 0) // top_count, axis=0)
    return jnp.where((source >= 0)[:, None], picked_rows, jnp.zeros((), tokens.dtype))


def send_rows(slot_rows):
    return lax.all_to_all(slot_rows, ("gx", "gy"), split_axis=0, concat_axis=0, tiled=True)


def on_device(tokens, expert_ids, backup_ids, scores, gate_weight, up_weight, down_weight):
    device_count = lax.axis_size(("gx", "gy"))
    own_index = lax.axis_index(("gx", "gy"))
    tok_rows, top_count = expert_ids.shape
    model_width = tokens.shape[1]
    per_source = tok_rows * top_count
    spare_quota = max(1, per_source // (4 * device_count))
    most_rows = max(2, (3 * per_source + 2 * device_count - 1) // (2 * device_count))
    first_flat = expert_ids.reshape(-1)
    backup_flat = backup_ids.reshape(-1)
    everyone = jnp.ones((per_source,), dtype=bool)
    first_within, first_table = ranks_within(first_flat, everyone, device_count)
    own_counts = jnp.sum(first_table, axis=0)
    all_counts = lax.all_gather(own_counts[None, :], ("gx", "gy"), axis=0, tiled=True)
    before = earlier_total(all_counts)
    own_before = lax.dynamic_index_in_dim(before, own_index, 0, keepdims=False)
    first_rank = jnp.sum(first_table * own_before[None, :], axis=1) + first_within
    kept_mask = first_rank < per_source
    spilled = jnp.logical_not(kept_mask)
    spill_rank = ranks_within(backup_flat, spilled, device_count)[0]
    spare_mask = spilled & (spill_rank < spare_quota)
    send_first = pack_rows(
        tokens,
        first_flat * most_rows + first_within,
        kept_mask,
        device_count * most_rows,
        top_count,
    ).reshape(device_count, most_rows, model_width)
    send_spill = pack_rows(
        tokens,
        backup_flat * spare_quota + spill_rank,
        spare_mask,
        device_count * spare_quota,
        top_count,
    ).reshape(device_count, spare_quota, model_width)
    recv_first = send_rows(send_first)
    recv_spill = send_rows(send_spill)
    count_column = lax.dynamic_index_in_dim(all_counts, own_index, 1, keepdims=False)
    before_column = lax.dynamic_index_in_dim(before, own_index, 1, keepdims=False)
    ending = before_column + count_column
    row_number = jnp.arange(per_source, dtype=jnp.int32)
    source_of_row = jnp.sum((ending[None, :] <= row_number[:, None]).astype(jnp.int32), axis=1)
    owner_grid = source_of_row[:, None] == jnp.arange(device_count, dtype=jnp.int32)[None, :]
    start_of_row = jnp.sum(jnp.where(owner_grid, before_column[None, :], 0), axis=1)
    filled = row_number < ending[device_count - 1]
    slot_index = jnp.minimum(source_of_row, device_count - 1) * most_rows + jnp.clip(
        row_number - start_of_row, 0, most_rows - 1
    )
    first_rows = jnp.take(
        recv_first.reshape(device_count * most_rows, model_width), slot_index, axis=0
    )
    first_rows = jnp.where(filled[:, None], first_rows, jnp.zeros((), first_rows.dtype))
    expert_rows = jnp.concatenate(
        [first_rows, recv_spill.reshape(device_count * spare_quota, model_width)], axis=0
    )
    gate = jnp.dot(expert_rows, gate_weight[0], preferred_element_type=jnp.float32)
    upward = jnp.dot(expert_rows, up_weight[0], preferred_element_type=jnp.float32)
    hidden = (jax.nn.silu(gate) * upward).astype(jnp.bfloat16)
    expert_out = jnp.dot(hidden, down_weight[0], preferred_element_type=jnp.float32).astype(
        jnp.bfloat16
    )
    position = jnp.arange(most_rows, dtype=jnp.int32)
    rank_grid = before_column[:, None] + position[None, :]
    live_slot = (position[None, :] < count_column[:, None]) & (rank_grid < per_source)
    back_first = jnp.take(expert_out[:per_source], jnp.clip(rank_grid, 0, per_source - 1), axis=0)
    back_first = jnp.where(live_slot[:, :, None], back_first, jnp.zeros((), back_first.dtype))
    back_spill = expert_out[per_source:].reshape(device_count, spare_quota, model_width)
    home_first = send_rows(back_first)
    home_spill = send_rows(back_spill)
    first_slot = jnp.minimum(first_flat * most_rows + first_within, device_count * most_rows - 1)
    spill_slot = backup_flat * spare_quota + jnp.minimum(spill_rank, spare_quota - 1)
    picked_first = jnp.take(
        home_first.reshape(device_count * most_rows, model_width), first_slot, axis=0
    )
    picked_spill = jnp.take(
        home_spill.reshape(device_count * spare_quota, model_width), spill_slot, axis=0
    )
    picked = jnp.where(kept_mask[:, None], picked_first, picked_spill).reshape(
        tok_rows, top_count, model_width
    )
    route_weights = scores / jnp.sum(scores, axis=1, keepdims=True)
    weights = jnp.where(
        (kept_mask | spare_mask).reshape(tok_rows, top_count),
        route_weights,
        jnp.zeros((), jnp.float32),
    )
    mixed = jnp.sum(weights[:, :, None] * picked.astype(jnp.float32), axis=1)
    return mixed.astype(jnp.bfloat16)


def exchange(cfg, tok_ref, ids_ref, backups_ref, scores_ref, gate_hbm, up_hbm, down_hbm, out_ref,
             flipped, before, near, metas, toks, wg, wu, wd, pick, comb, gate, upward, hidden,
             own, to_core, from_core, to_one, from_one, to_two, from_two, to_z, from_z,
             meta_send, meta_recv, ag_send, ag_recv, rs_send, rs_recv, w_sem):
    chunks, first_sends, order, experts, cap, quota, slots, top = cfg
    halves = [chunk[0] for chunk in chunks]
    z_last = [chunk[1] for chunk in chunks]
    count = len(chunks)
    starts = [2 * sum(halves[:k]) for k in range(count)]
    columns = [pl.ds(starts[k], 2 * halves[k]) for k in range(count)]
    side = [[pl.ds(0, half), pl.ds(half, half)] for half in halves]
    bf16, f32 = jnp.bfloat16, jnp.float32
    z = lax.axis_index("gx")
    g = lax.axis_index("gy")
    c = lax.rem(g, 2)
    x = lax.rem(lax.div(g, 2), 2)
    y = lax.div(g, 4)
    core_peer = (z, g + 1 - 2 * c)
    x_peer = (z, g + 2 - 4 * x)
    y_peer = (z, g + 4 - 8 * y)
    far_peer = (z, 6 - 4 * y - 2 * x + c)
    planes = [z, z + 1 - 2 * lax.rem(z, 2), z + 2 - 4 * lax.div(z, 2), 3 - z]
    z_peers = [(there, g) for there in planes[1:]]
    expert = z * 8 + g

    def remote(src, dst, send, recv, device):
        return pltpu.make_async_remote_copy(
            src_ref=src, dst_ref=dst, send_sem=send, recv_sem=recv,
            device_id=device, device_id_type=pl.DeviceIdType.MESH)

    barrier = pltpu.get_barrier_semaphore()
    for peer in [core_peer, x_peer, y_peer, far_peer] + z_peers:
        pl.semaphore_signal(barrier, inc=1, device_id=peer, device_id_type=pl.DeviceIdType.MESH)

    weight_copies = []
    for k in range(count):
        pair = [pltpu.make_async_copy(gate_hbm.at[0, columns[k]], wg.at[columns[k]], w_sem.at[0, k]),
                pltpu.make_async_copy(up_hbm.at[0, columns[k]], wu.at[columns[k]], w_sem.at[1, k])]
        weight_copies.append(pair)
        for copy in pair:
            copy.start()
    down_copies = []
    for k in range(count):
        copy = pltpu.make_async_copy(down_hbm.at[0, :, columns[k]], wd[k], w_sem.at[2, k])
        copy.start()
        down_copies.append(copy)

    scores = scores_ref[...]
    flipped[0:3 * top, 0:16] = jnp.concatenate(
        [ids_ref[...].astype(f32), backups_ref[...].astype(f32),
         scores / jnp.sum(scores, axis=0, keepdims=True)], axis=0)
    metas[z, y, x, c] = flipped[...].T[0:16]
    for k in range(count):
        toks[k][z, y, x, c] = tok_ref[:, starts[k]:starts[k] + 2 * halves[k]]
    row = lax.broadcasted_iota(jnp.int32, (512, 512), 0)
    col = lax.broadcasted_iota(jnp.int32, (512, 512), 1)
    before[...] = jnp.where(row < col, 1.0, 0.0).astype(bf16)
    same = lax.shift_right_logical(row, 4) == lax.shift_right_logical(col, 4)
    near[...] = jnp.where(same & (row < col), 1.0, 0.0).astype(bf16)
    pl.semaphore_wait(barrier, 7)

    started = []

    def begin(copy):
        copy.start()
        started.append(copy)

    meta_parts = [metas.at[z, y, x, c]] * 3 + [metas.at[:, y, x, c]] * 3 + [metas.at[:, :, :, c]]
    meta_peers = z_peers + [x_peer, y_peer, far_peer, core_peer]
    metas_out = [remote(meta_parts[i], meta_parts[i], meta_send.at[i], meta_recv.at[i], meta_peers[i])
                 for i in range(7)]

    def gather_copies(k):
        buf, table = toks[k], {}
        sem = lambda at: (ag_send.at[k, at], ag_recv.at[k, at])
        for b, there in enumerate(planes):
            whole = buf.at[there, :, :, c]
            for flip in range(2):
                line = buf.at[there, y, x, c, :, side[k][flip]]
                plane = (buf.at[there, :, x, c, :, side[k][1]] if flip else buf.at[there, y, :, c, :, side[k][0]])
                one, two = (y_peer, x_peer) if flip else (x_peer, y_peer)
                table[0, b, flip] = remote(line, line, *sem(6 * b + flip), one)
                table[1, b, flip] = remote(plane, plane, *sem(6 * b + 2 + flip), two)
            table[2, b] = remote(whole, whole, *sem(6 * b + 4), core_peer)
            if b:
                mine = buf.at[z, :, :, c] if z_last[k] else buf.at[z, y, x, c]
                table[3, b] = remote(mine, mine, *sem(6 * b + 5), z_peers[b - 1])
        return table

    gathers = [gather_copies(k) for k in range(count)]

    def route():
        record = metas[...].reshape(512, 128).T
        first, backup, weight = record[0:top], record[top:2 * top], record[2 * top:3 * top]
        number = lax.broadcasted_iota(jnp.int32, (experts, 512), 0).astype(f32)
        named = jnp.zeros((experts, 512), f32)
        for k in range(top):
            named += jnp.where(first[k:k + 1] == number, 1.0, 0.0)
        rank = jnp.dot(named.astype(bf16), before[...], preferred_element_type=f32)
        spilled = jnp.where(rank >= cap, named, 0.0)
        me = expert.astype(f32)
        is_me = jnp.where(number == me, 1.0, 0.0)
        total = lambda table: jnp.sum(table, axis=0, keepdims=True)
        my_named = total(is_me * named)
        my_rank = total(is_me * rank)
        my_weight = total(jnp.where(first == me, weight, 0.0))
        has_backup = total(jnp.where(backup == me, 1.0, 0.0))
        its_first = total(jnp.where(backup == me, first, 0.0))
        its_weight = total(jnp.where(backup == me, weight, 0.0))
        moved = has_backup * total(jnp.where(number == its_first, spilled, 0.0))
        moved_wide = jnp.broadcast_to(moved, (16, 512))
        spill_rank = jnp.dot(moved_wide.astype(bf16), near[...], preferred_element_type=f32)[0:1]
        token = lax.broadcasted_iota(jnp.int32, (1, 512), 1)
        block = lax.shift_right_logical(token, 4).astype(f32)
        kept_slot = lax.broadcasted_iota(jnp.int32, (cap, 512), 0).astype(f32)
        spare_slot = lax.broadcasted_iota(jnp.int32, (slots - cap, 512), 0).astype(f32)
        spare_at = jnp.where(spill_rank < quota, block * quota + spill_rank, -1.0)
        kept_grid = jnp.where(my_rank == kept_slot, my_named, 0.0)
        spare_grid = jnp.where(spare_at == spare_slot, moved, 0.0)
        pick[...] = jnp.concatenate([kept_grid, spare_grid], axis=0).astype(bf16)
        mixing = jnp.concatenate([kept_grid * my_weight, spare_grid * its_weight], axis=0)
        comb[...] = mixing.T.astype(bf16).reshape(16, 2, 16, slots)

    def meta_step(i):
        waits, sends = ((range(0, 3), range(3, 6)), (range(3, 6), range(6, 7)), (range(6, 7), ()))[i]
        for at in waits:
            metas_out[at].wait_recv()
        for at in sends:
            begin(metas_out[at])
        if i == 2:
            route()

    def gather_step(stage, k, b):
        if z_last[k] and b > 0 or stage == 0:
            gathers[k][3, b].wait_recv()
        else:
            for flip in range(2):
                gathers[k][stage - 1, b, flip].wait_recv()
        if stage < 2:
            for flip in range(2):
                begin(gathers[k][stage, b, flip])
            return
        if z_last[k] and b == 0:
            for other in range(1, 4):
                begin(gathers[k][3, other])
        begin(gathers[k][2, b])

    projected = []

    def project(k):
        for b in range(4):
            gathers[k][2, b].wait_recv()
        for copy in weight_copies[k]:
            copy.wait()
        rows = jnp.dot(pick[...], toks[k][...].reshape(512, 2 * halves[k]), preferred_element_type=f32).astype(bf16)
        new_gate = jnp.dot(rows, wg[columns[k], :], preferred_element_type=f32)
        new_up = jnp.dot(rows, wu[columns[k], :], preferred_element_type=f32)
        projected.append(k)
        if len(projected) == 1:
            gate[...] = new_gate
            upward[...] = new_up
        elif len(projected) < count:
            gate[...] += new_gate
            upward[...] += new_up
        else:
            full = gate[...] + new_gate
            hidden[...] = (full / (1.0 + jnp.exp(-full)) * (upward[...] + new_up)).astype(bf16)

    def scatter_copies(k):
        table = {}
        sem = lambda at: (rs_send.at[k, at], rs_recv.at[k, at])
        for b, there in enumerate(planes):
            for flip in range(2):
                one, two = (x_peer, y_peer) if flip else (y_peer, x_peer)
                table[0, b, flip] = remote(to_one[k].at[flip, there], from_one[k].at[flip, there],
                                           *sem(5 * b + flip), one)
                table[1, b, flip] = remote(to_two[k].at[flip, there], from_two[k].at[flip, there],
                                           *sem(5 * b + 2 + flip), two)
            if b:
                table[2, b] = remote(to_z[k].at[b - 1], from_z[k].at[b - 1], *sem(5 * b + 4), z_peers[b - 1])
        return table

    cores = [remote(to_core[k], from_core[k], rs_send.at[k, 4], rs_recv.at[k, 4], core_peer) for k in range(count)]
    scatters = [scatter_copies(k) for k in range(count)]

    def produce(k):
        down_copies[k].wait()
        rows = jnp.dot(hidden[...], wd[k][...], preferred_element_type=f32).astype(bf16)
        sides = jnp.concatenate([comb[:, 1 - c].reshape(256, slots), comb[:, c].reshape(256, slots)], axis=0)
        mixed = jnp.dot(sides, rows, preferred_element_type=f32)
        to_core[k][...] = mixed[:256].astype(bf16).reshape(4, 2, 2, 16, 2 * halves[k])
        begin(cores[k])
        own[k][...] = mixed[256:].reshape(4, 2, 2, 16, 2 * halves[k])

    def at_one(k, flip, zz, first, second):
        yy, xx = (second, first) if flip else (first, second)
        mine = own[k][zz, yy, xx, :, side[k][flip]]
        if z_last[k]:
            return mine
        return mine + from_core[k][zz, yy, xx, :, side[k][flip]].astype(f32)

    def at_two(k, flip, zz, first, second):
        return at_one(k, flip, zz, first, second) + from_one[k][flip, zz, second].astype(f32)

    def at_z(k, flip, zz):
        first, second = (x, y) if flip else (y, x)
        return at_two(k, flip, zz, first, second) + from_two[k][flip, zz].astype(f32)

    joined = []

    def scatter_step(stage, k, b):
        there = planes[b]
        if k not in joined:
            joined.append(k)
            cores[k].wait_recv()
        if stage == 3:
            for other in (3, 2, 1):
                total = own[k][planes[other]] + from_core[k][planes[other]].astype(f32)
                to_z[k][other - 1] = total.astype(bf16)
                begin(scatters[k][2, other])
            return
        if stage == 0 and z_last[k]:
            total = own[k][z] + from_core[k][z].astype(f32)
            for other in range(1, 4):
                scatters[k][2, other].wait_recv()
                total += from_z[k][other - 1].astype(f32)
            own[k][z] = total
        for flip in range(2):
            first, second = (x, y) if flip else (y, x)
            if stage == 0:
                for other in range(2):
                    to_one[k][flip, there, other] = at_one(k, flip, there, 1 - first, other).astype(bf16)
            elif stage == 1:
                scatters[k][0, b, flip].wait_recv()
                to_two[k][flip, there] = at_two(k, flip, there, first, 1 - second).astype(bf16)
            else:
                scatters[k][1, b, flip].wait_recv()
                to_z[k][b - 1, :, side[k][flip]] = at_z(k, flip, there).astype(bf16)
            if stage < 2:
                begin(scatters[k][stage, b, flip])
        if stage == 2:
            begin(scatters[k][2, b])

    def finish(k):
        if not z_last[k]:
            for b in range(1, 4):
                scatters[k][2, b].wait_recv()
        for flip in range(2):
            scatters[k][1, 0, flip].wait_recv()
            total = at_z(k, flip, z)
            if not z_last[k]:
                for b in range(1, 4):
                    total += from_z[k][b - 1, :, side[k][flip]].astype(f32)
            start = starts[k] + flip * halves[k]
            out_ref[:, start:start + halves[k]] = total.astype(bf16)

    for copy in metas_out[0:3]:
        begin(copy)
    for stage, k, at in first_sends:
        begin(gathers[k][3, at] if stage else gathers[k][0, 0, at])
    for event in order:
        kind, at = event[0], event[1:]
        if kind == META:
            meta_step(*at)
        elif kind == GATHER:
            gather_step(*at)
        elif kind == PROJECT:
            project(*at)
        elif kind == PRODUCE:
            produce(*at)
        elif kind == SCATTER:
            scatter_step(*at)
        else:
            finish(*at)

    for copy in started:
        copy.wait_send()


def fused_body(chunks, first_sends, order, tokens, expert_ids, backup_ids, scores, gate_weight, up_weight, down_weight):
    device_count = lax.axis_size(("gx", "gy"))
    tok_rows, top = expert_ids.shape
    model, ff = gate_weight.shape[1:]
    cap = tok_rows * top
    quota = max(1, cap // (4 * device_count))
    slots = cap + device_count * quota
    count = len(chunks)
    bf16, f32 = jnp.bfloat16, jnp.float32
    grid = (4, 2, 2)
    vmem = lambda shape, kind: pltpu.VMEM(shape, kind)
    pairs = lambda lead, kind: tuple(vmem(lead + (tok_rows, 2 * half), kind) for half, _ in chunks)
    each = lambda lead, kind: tuple(vmem((2,) + lead + (tok_rows, half), kind) for half, _ in chunks)
    to_planes = tuple(
        vmem(((3, 2, 2) if z_last else (3,)) + (tok_rows, 2 * half), bf16) for half, z_last in chunks)
    scratch = [
        vmem((128, 128), f32), vmem((512, 512), bf16), vmem((512, 512), bf16), vmem(grid + (2, tok_rows, 128), f32),
        pairs(grid + (2,), bf16),
        vmem((model, ff), bf16), vmem((model, ff), bf16), tuple(vmem((ff, 2 * half), bf16) for half, _ in chunks),
        vmem((slots, 512), bf16), vmem((16, 2, tok_rows, slots), bf16),
        vmem((slots, ff), f32), vmem((slots, ff), f32), vmem((slots, ff), bf16),
        pairs(grid, f32), pairs(grid, bf16), pairs(grid, bf16),
        each((4, 2), bf16), each((4, 2), bf16), each((4,), bf16), each((4,), bf16), to_planes, to_planes,
        pltpu.SemaphoreType.DMA((7,)), pltpu.SemaphoreType.DMA((7,)),
        pltpu.SemaphoreType.DMA((count, 24)), pltpu.SemaphoreType.DMA((count, 24)),
        pltpu.SemaphoreType.DMA((count, 20)), pltpu.SemaphoreType.DMA((count, 20)),
        pltpu.SemaphoreType.DMA((3, count)),
    ]
    whole = pl.BlockSpec(memory_space=pltpu.VMEM)
    away = pl.BlockSpec(memory_space=pl.ANY)
    return pl.pallas_call(
        functools.partial(exchange, (chunks, first_sends, order, device_count, cap, quota, slots, top)),
        out_shape=jax.ShapeDtypeStruct((tok_rows, model), bf16),
        in_specs=[whole, whole, whole, whole, away, away, away],
        out_specs=whole,
        scratch_shapes=scratch,
        compiler_params=pltpu.CompilerParams(
            collective_id=0, has_side_effects=True, vmem_limit_bytes=60 * 1024 * 1024),
    )(tokens, expert_ids.T, backup_ids.T, scores.T, gate_weight, up_weight, down_weight)


META, GATHER, PROJECT, PRODUCE, SCATTER, FINISH = range(6)
CHUNKS = ((768, 0), (768, 0), (256, 1))
FIRST = (
    (3, 0, 1), (0, 2, 0), (0, 2, 1), (3, 0, 2), (3, 1, 2), (0, 1, 1), (0, 0, 1), (3, 1, 1), (0, 1, 0),
    (3, 0, 3), (3, 1, 3), (0, 0, 0),
)
ORDER = (
    (GATHER, 1, 2, 0), (META, 0), (GATHER, 0, 0, 1), (GATHER, 1, 0, 0), (GATHER, 0, 0, 2), (GATHER, 1, 1, 0),
    (META, 1), (GATHER, 0, 1, 1), (GATHER, 0, 1, 2), (GATHER, 1, 0, 1), (GATHER, 2, 2, 0), (GATHER, 0, 0, 3),
    (GATHER, 1, 0, 2), (META, 2), (GATHER, 0, 1, 3), (GATHER, 1, 1, 1), (GATHER, 2, 2, 1), (GATHER, 1, 0, 3),
    (GATHER, 2, 1, 0), (GATHER, 1, 1, 3), (GATHER, 2, 0, 2), (GATHER, 2, 1, 1), (GATHER, 1, 1, 2),
    (GATHER, 2, 0, 0), (GATHER, 2, 0, 1), (GATHER, 2, 0, 3), (GATHER, 2, 2, 3), (GATHER, 2, 2, 2),
    (GATHER, 2, 1, 3), (PROJECT, 0), (GATHER, 2, 1, 2), (PROJECT, 2), (PROJECT, 1), (PRODUCE, 0), (PRODUCE, 2),
    (SCATTER, 0, 0, 3), (SCATTER, 0, 0, 1), (SCATTER, 0, 0, 2), (SCATTER, 3, 2, 0), (PRODUCE, 1),
    (SCATTER, 0, 0, 0), (SCATTER, 1, 0, 3), (SCATTER, 0, 1, 3), (SCATTER, 1, 0, 2), (SCATTER, 0, 1, 2),
    (SCATTER, 0, 1, 1), (SCATTER, 2, 0, 3), (SCATTER, 1, 1, 3), (SCATTER, 2, 0, 2), (SCATTER, 1, 0, 1),
    (SCATTER, 1, 1, 2), (SCATTER, 0, 2, 0), (SCATTER, 0, 1, 0), (SCATTER, 1, 1, 1), (SCATTER, 2, 1, 3),
    (SCATTER, 1, 0, 0), (SCATTER, 2, 0, 1), (SCATTER, 2, 1, 2), (SCATTER, 1, 1, 0), (SCATTER, 1, 2, 0),
    (SCATTER, 2, 1, 1), (FINISH, 0), (FINISH, 2), (FINISH, 1),
)


def pick_body(mesh):
    if mesh.shape["gx"] == 4 and mesh.shape["gy"] == 8:
        return functools.partial(fused_body, CHUNKS, FIRST, ORDER)
    return on_device


def solution(mesh):
    placed = (
        P(("gx", "gy"), None),
        P(("gx", "gy"), None),
        P(("gx", "gy"), None),
        P(("gx", "gy"), None),
        P(("gx", "gy"), None, None),
        P(("gx", "gy"), None, None),
        P(("gx", "gy"), None, None),
    )
    return jax.shard_map(
        pick_body(mesh), mesh=mesh, in_specs=placed, out_specs=P(("gx", "gy"), None), check_vma=False
    )
```

```python
import functools
import jax
import jax.numpy as jnp
from jax import lax
from jax.experimental import pallas as pl
from jax.experimental.pallas import tpu as pltpu
from jax.sharding import PartitionSpec as P


def earlier_total(table):
    row = lax.broadcasted_iota(jnp.int32, (table.shape[0],) * 2, 0)
    col = lax.broadcasted_iota(jnp.int32, (table.shape[0],) * 2, 1)
    lower = (col < row).astype(jnp.bfloat16)
    total = jnp.dot(lower, table.astype(jnp.bfloat16), preferred_element_type=jnp.float32)
    return total.astype(jnp.int32)


def ranks_within(numbers, active, expert_count):
    table = (
        (numbers[:, None] == jnp.arange(expert_count, dtype=jnp.int32)[None, :]) & active[:, None]
    ).astype(jnp.int32)
    within = jnp.sum(earlier_total(table) * table, axis=1)
    return (within, table)


def pack_rows(tokens, destination, active, slot_total, top_count):
    pick_number = jnp.arange(destination.shape[0], dtype=jnp.int32)
    match_grid = (
        destination[None, :] == jnp.arange(slot_total, dtype=jnp.int32)[:, None]
    ) & active[None, :]
    source = jnp.sum(jnp.where(match_grid, pick_number[None, :] + 1, 0), axis=1) - 1
    picked_rows = jnp.take(tokens, jnp.maximum(source, 0) // top_count, axis=0)
    return jnp.where((source >= 0)[:, None], picked_rows, jnp.zeros((), tokens.dtype))


def send_rows(slot_rows):
    return lax.all_to_all(slot_rows, ("gx", "gy"), split_axis=0, concat_axis=0, tiled=True)


def on_device(tokens, expert_ids, backup_ids, scores, gate_weight, up_weight, down_weight):
    device_count = lax.axis_size(("gx", "gy"))
    own_index = lax.axis_index(("gx", "gy"))
    tok_rows, top_count = expert_ids.shape
    model_width = tokens.shape[1]
    per_source = tok_rows * top_count
    spare_quota = max(1, per_source // (4 * device_count))
    most_rows = max(2, (3 * per_source + 2 * device_count - 1) // (2 * device_count))
    first_flat = expert_ids.reshape(-1)
    backup_flat = backup_ids.reshape(-1)
    everyone = jnp.ones((per_source,), dtype=bool)
    first_within, first_table = ranks_within(first_flat, everyone, device_count)
    own_counts = jnp.sum(first_table, axis=0)
    all_counts = lax.all_gather(own_counts[None, :], ("gx", "gy"), axis=0, tiled=True)
    before = earlier_total(all_counts)
    own_before = lax.dynamic_index_in_dim(before, own_index, 0, keepdims=False)
    first_rank = jnp.sum(first_table * own_before[None, :], axis=1) + first_within
    kept_mask = first_rank < per_source
    spilled = jnp.logical_not(kept_mask)
    spill_rank = ranks_within(backup_flat, spilled, device_count)[0]
    spare_mask = spilled & (spill_rank < spare_quota)
    send_first = pack_rows(
        tokens,
        first_flat * most_rows + first_within,
        kept_mask,
        device_count * most_rows,
        top_count,
    ).reshape(device_count, most_rows, model_width)
    send_spill = pack_rows(
        tokens,
        backup_flat * spare_quota + spill_rank,
        spare_mask,
        device_count * spare_quota,
        top_count,
    ).reshape(device_count, spare_quota, model_width)
    recv_first = send_rows(send_first)
    recv_spill = send_rows(send_spill)
    count_column = lax.dynamic_index_in_dim(all_counts, own_index, 1, keepdims=False)
    before_column = lax.dynamic_index_in_dim(before, own_index, 1, keepdims=False)
    ending = before_column + count_column
    row_number = jnp.arange(per_source, dtype=jnp.int32)
    source_of_row = jnp.sum((ending[None, :] <= row_number[:, None]).astype(jnp.int32), axis=1)
    owner_grid = source_of_row[:, None] == jnp.arange(device_count, dtype=jnp.int32)[None, :]
    start_of_row = jnp.sum(jnp.where(owner_grid, before_column[None, :], 0), axis=1)
    filled = row_number < ending[device_count - 1]
    slot_index = jnp.minimum(source_of_row, device_count - 1) * most_rows + jnp.clip(
        row_number - start_of_row, 0, most_rows - 1
    )
    first_rows = jnp.take(
        recv_first.reshape(device_count * most_rows, model_width), slot_index, axis=0
    )
    first_rows = jnp.where(filled[:, None], first_rows, jnp.zeros((), first_rows.dtype))
    expert_rows = jnp.concatenate(
        [first_rows, recv_spill.reshape(device_count * spare_quota, model_width)], axis=0
    )
    gate = jnp.dot(expert_rows, gate_weight[0], preferred_element_type=jnp.float32)
    upward = jnp.dot(expert_rows, up_weight[0], preferred_element_type=jnp.float32)
    hidden = (jax.nn.silu(gate) * upward).astype(jnp.bfloat16)
    expert_out = jnp.dot(hidden, down_weight[0], preferred_element_type=jnp.float32).astype(
        jnp.bfloat16
    )
    position = jnp.arange(most_rows, dtype=jnp.int32)
    rank_grid = before_column[:, None] + position[None, :]
    live_slot = (position[None, :] < count_column[:, None]) & (rank_grid < per_source)
    back_first = jnp.take(expert_out[:per_source], jnp.clip(rank_grid, 0, per_source - 1), axis=0)
    back_first = jnp.where(live_slot[:, :, None], back_first, jnp.zeros((), back_first.dtype))
    back_spill = expert_out[per_source:].reshape(device_count, spare_quota, model_width)
    home_first = send_rows(back_first)
    home_spill = send_rows(back_spill)
    first_slot = jnp.minimum(first_flat * most_rows + first_within, device_count * most_rows - 1)
    spill_slot = backup_flat * spare_quota + jnp.minimum(spill_rank, spare_quota - 1)
    picked_first = jnp.take(
        home_first.reshape(device_count * most_rows, model_width), first_slot, axis=0
    )
    picked_spill = jnp.take(
        home_spill.reshape(device_count * spare_quota, model_width), spill_slot, axis=0
    )
    picked = jnp.where(kept_mask[:, None], picked_first, picked_spill).reshape(
        tok_rows, top_count, model_width
    )
    route_weights = scores / jnp.sum(scores, axis=1, keepdims=True)
    weights = jnp.where(
        (kept_mask | spare_mask).reshape(tok_rows, top_count),
        route_weights,
        jnp.zeros((), jnp.float32),
    )
    mixed = jnp.sum(weights[:, :, None] * picked.astype(jnp.float32), axis=1)
    return mixed.astype(jnp.bfloat16)


def exchange(cfg, tok_hbm, ids_hbm, backups_hbm, scores_hbm, gate_hbm, up_hbm, down_hbm, out_ref,
             ids_ref, backups_ref, scores_ref, in_sem, flipped, before, near, metas, toks, wg, wu, wd, pick, comb, gate, upward, hidden,
             own, to_core, from_core, to_one, from_one, to_two, from_two, to_z, from_z,
             meta_send, meta_recv, ag_send, ag_recv, rs_send, rs_recv, w_sem):
    chunks, first_sends, order, experts, cap, quota, slots, top = cfg
    halves = [chunk[0] for chunk in chunks]
    z_last = [chunk[1] for chunk in chunks]
    count = len(chunks)
    starts = [2 * sum(halves[:k]) for k in range(count)]
    columns = [pl.ds(starts[k], 2 * halves[k]) for k in range(count)]
    side = [[pl.ds(0, half), pl.ds(half, half)] for half in halves]
    bf16, f32 = jnp.bfloat16, jnp.float32
    z = lax.axis_index("gx")
    g = lax.axis_index("gy")
    c = lax.rem(g, 2)
    x = lax.rem(lax.div(g, 2), 2)
    y = lax.div(g, 4)
    core_peer = (z, g + 1 - 2 * c)
    x_peer = (z, g + 2 - 4 * x)
    y_peer = (z, g + 4 - 8 * y)
    far_peer = (z, 6 - 4 * y - 2 * x + c)
    planes = [z, z + 1 - 2 * lax.rem(z, 2), z + 2 - 4 * lax.div(z, 2), 3 - z]
    z_peers = [(there, g) for there in planes[1:]]
    expert = z * 8 + g

    def remote(src, dst, send, recv, device):
        return pltpu.make_async_remote_copy(
            src_ref=src, dst_ref=dst, send_sem=send, recv_sem=recv,
            device_id=device, device_id_type=pl.DeviceIdType.MESH)

    barrier = pltpu.get_barrier_semaphore()
    for peer in [core_peer, x_peer, y_peer, far_peer] + z_peers:
        pl.semaphore_signal(barrier, inc=1, device_id=peer, device_id_type=pl.DeviceIdType.MESH)

    small_copies = [pltpu.make_async_copy(src, dst, in_sem.at[i]) for i, (src, dst) in enumerate(
        ((ids_hbm, ids_ref), (backups_hbm, backups_ref), (scores_hbm, scores_ref)))]
    token_copies = [pltpu.make_async_copy(tok_hbm.at[:, columns[k]], toks[k].at[z, y, x, c], in_sem.at[3 + k])
                    for k in range(count)]
    for copy in small_copies + token_copies:
        copy.start()
    for copy in small_copies + token_copies:
        copy.wait()
    weight_copies = []
    for k in range(count):
        pair = [pltpu.make_async_copy(gate_hbm.at[0, columns[k]], wg.at[columns[k]], w_sem.at[0, k]),
                pltpu.make_async_copy(up_hbm.at[0, columns[k]], wu.at[columns[k]], w_sem.at[1, k])]
        weight_copies.append(pair)
        for copy in pair:
            copy.start()
    down_copies = []
    for k in range(count):
        copy = pltpu.make_async_copy(down_hbm.at[0, :, columns[k]], wd[k], w_sem.at[2, k])
        copy.start()
        down_copies.append(copy)

    scores = scores_ref[...]
    flipped[0:3 * top, 0:16] = jnp.concatenate(
        [ids_ref[...].astype(f32), backups_ref[...].astype(f32),
         scores / jnp.sum(scores, axis=0, keepdims=True)], axis=0)
    metas[z, y, x, c] = flipped[...].T[0:16]
    row = lax.broadcasted_iota(jnp.int32, (512, 512), 0)
    col = lax.broadcasted_iota(jnp.int32, (512, 512), 1)
    before[...] = jnp.where(row < col, 1.0, 0.0).astype(bf16)
    same = lax.shift_right_logical(row, 4) == lax.shift_right_logical(col, 4)
    near[...] = jnp.where(same & (row < col), 1.0, 0.0).astype(bf16)
    pl.semaphore_wait(barrier, 7)

    started = []

    def begin(copy):
        copy.start()
        started.append(copy)

    meta_parts = [metas.at[z, y, x, c]] * 3 + [metas.at[:, y, x, c]] * 3 + [metas.at[:, :, :, c]]
    meta_peers = z_peers + [x_peer, y_peer, far_peer, core_peer]
    metas_out = [remote(meta_parts[i], meta_parts[i], meta_send.at[i], meta_recv.at[i], meta_peers[i])
                 for i in range(7)]

    def gather_copies(k):
        buf, table = toks[k], {}
        sem = lambda at: (ag_send.at[k, at], ag_recv.at[k, at])
        for b, there in enumerate(planes):
            whole = buf.at[there, :, :, c]
            for flip in range(2):
                line = buf.at[there, y, x, c, :, side[k][flip]]
                plane = (buf.at[there, :, x, c, :, side[k][1]] if flip else buf.at[there, y, :, c, :, side[k][0]])
                one, two = (y_peer, x_peer) if flip else (x_peer, y_peer)
                table[0, b, flip] = remote(line, line, *sem(6 * b + flip), one)
                table[1, b, flip] = remote(plane, plane, *sem(6 * b + 2 + flip), two)
            table[2, b] = remote(whole, whole, *sem(6 * b + 4), core_peer)
            if b:
                mine = buf.at[z, :, :, c] if z_last[k] else buf.at[z, y, x, c]
                table[3, b] = remote(mine, mine, *sem(6 * b + 5), z_peers[b - 1])
        return table

    gathers = [gather_copies(k) for k in range(count)]

    def route():
        record = metas[...].reshape(512, 128).T
        first, backup, weight = record[0:top], record[top:2 * top], record[2 * top:3 * top]
        number = lax.broadcasted_iota(jnp.int32, (experts, 512), 0).astype(f32)
        named = jnp.zeros((experts, 512), f32)
        for k in range(top):
            named += jnp.where(first[k:k + 1] == number, 1.0, 0.0)
        rank = jnp.dot(named.astype(bf16), before[...], preferred_element_type=f32)
        spilled = jnp.where(rank >= cap, named, 0.0)
        me = expert.astype(f32)
        is_me = jnp.where(number == me, 1.0, 0.0)
        total = lambda table: jnp.sum(table, axis=0, keepdims=True)
        my_named = total(is_me * named)
        my_rank = total(is_me * rank)
        my_weight = total(jnp.where(first == me, weight, 0.0))
        has_backup = total(jnp.where(backup == me, 1.0, 0.0))
        its_first = total(jnp.where(backup == me, first, 0.0))
        its_weight = total(jnp.where(backup == me, weight, 0.0))
        moved = has_backup * total(jnp.where(number == its_first, spilled, 0.0))
        moved_wide = jnp.broadcast_to(moved, (16, 512))
        spill_rank = jnp.dot(moved_wide.astype(bf16), near[...], preferred_element_type=f32)[0:1]
        token = lax.broadcasted_iota(jnp.int32, (1, 512), 1)
        block = lax.shift_right_logical(token, 4).astype(f32)
        kept_slot = lax.broadcasted_iota(jnp.int32, (cap, 512), 0).astype(f32)
        spare_slot = lax.broadcasted_iota(jnp.int32, (slots - cap, 512), 0).astype(f32)
        spare_at = jnp.where(spill_rank < quota, block * quota + spill_rank, -1.0)
        kept_grid = jnp.where(my_rank == kept_slot, my_named, 0.0)
        spare_grid = jnp.where(spare_at == spare_slot, moved, 0.0)
        pick[...] = jnp.concatenate([kept_grid, spare_grid], axis=0).astype(bf16)
        mixing = jnp.concatenate([kept_grid * my_weight, spare_grid * its_weight], axis=0)
        comb[...] = mixing.T.astype(bf16).reshape(16, 2, 16, slots)

    def meta_step(i):
        waits, sends = ((range(0, 3), range(3, 6)), (range(3, 6), range(6, 7)), (range(6, 7), ()))[i]
        for at in waits:
            metas_out[at].wait_recv()
        for at in sends:
            begin(metas_out[at])
        if i == 2:
            route()

    def gather_step(stage, k, b):
        if z_last[k] and b > 0 or stage == 0:
            gathers[k][3, b].wait_recv()
        else:
            for flip in range(2):
                gathers[k][stage - 1, b, flip].wait_recv()
        if stage < 2:
            for flip in range(2):
                begin(gathers[k][stage, b, flip])
            return
        if z_last[k] and b == 0:
            for other in range(1, 4):
                begin(gathers[k][3, other])
        begin(gathers[k][2, b])

    projected = []

    def project(k):
        for b in range(4):
            gathers[k][2, b].wait_recv()
        for copy in weight_copies[k]:
            copy.wait()
        rows = jnp.dot(pick[...], toks[k][...].reshape(512, 2 * halves[k]), preferred_element_type=f32).astype(bf16)
        new_gate = jnp.dot(rows, wg[columns[k], :], preferred_element_type=f32)
        new_up = jnp.dot(rows, wu[columns[k], :], preferred_element_type=f32)
        projected.append(k)
        if len(projected) == 1:
            gate[...] = new_gate
            upward[...] = new_up
        elif len(projected) < count:
            gate[...] += new_gate
            upward[...] += new_up
        else:
            full = gate[...] + new_gate
            hidden[...] = (full / (1.0 + jnp.exp(-full)) * (upward[...] + new_up)).astype(bf16)

    def scatter_copies(k):
        table = {}
        sem = lambda at: (rs_send.at[k, at], rs_recv.at[k, at])
        for b, there in enumerate(planes):
            for flip in range(2):
                one, two = (x_peer, y_peer) if flip else (y_peer, x_peer)
                table[0, b, flip] = remote(to_one[k].at[flip, there], from_one[k].at[flip, there],
                                           *sem(5 * b + flip), one)
                table[1, b, flip] = remote(to_two[k].at[flip, there], from_two[k].at[flip, there],
                                           *sem(5 * b + 2 + flip), two)
            if b:
                table[2, b] = remote(to_z[k].at[b - 1], from_z[k].at[b - 1], *sem(5 * b + 4), z_peers[b - 1])
        return table

    cores = [remote(to_core[k], from_core[k], rs_send.at[k, 4], rs_recv.at[k, 4], core_peer) for k in range(count)]
    scatters = [scatter_copies(k) for k in range(count)]

    def produce(k):
        down_copies[k].wait()
        rows = jnp.dot(hidden[...], wd[k][...], preferred_element_type=f32).astype(bf16)
        sides = jnp.concatenate([comb[:, 1 - c].reshape(256, slots), comb[:, c].reshape(256, slots)], axis=0)
        mixed = jnp.dot(sides, rows, preferred_element_type=f32)
        to_core[k][...] = mixed[:256].astype(bf16).reshape(4, 2, 2, 16, 2 * halves[k])
        begin(cores[k])
        own[k][...] = mixed[256:].reshape(4, 2, 2, 16, 2 * halves[k])

    def at_one(k, flip, zz, first, second):
        yy, xx = (second, first) if flip else (first, second)
        mine = own[k][zz, yy, xx, :, side[k][flip]]
        if z_last[k]:
            return mine
        return mine + from_core[k][zz, yy, xx, :, side[k][flip]].astype(f32)

    def at_two(k, flip, zz, first, second):
        return at_one(k, flip, zz, first, second) + from_one[k][flip, zz, second].astype(f32)

    def at_z(k, flip, zz):
        first, second = (x, y) if flip else (y, x)
        return at_two(k, flip, zz, first, second) + from_two[k][flip, zz].astype(f32)

    joined = []

    def scatter_step(stage, k, b):
        there = planes[b]
        if k not in joined:
            joined.append(k)
            cores[k].wait_recv()
        if stage == 3:
            for other in (3, 2, 1):
                total = own[k][planes[other]] + from_core[k][planes[other]].astype(f32)
                to_z[k][other - 1] = total.astype(bf16)
                begin(scatters[k][2, other])
            return
        if stage == 0 and z_last[k]:
            total = own[k][z] + from_core[k][z].astype(f32)
            for other in range(1, 4):
                scatters[k][2, other].wait_recv()
                total += from_z[k][other - 1].astype(f32)
            own[k][z] = total
        for flip in range(2):
            first, second = (x, y) if flip else (y, x)
            if stage == 0:
                for other in range(2):
                    to_one[k][flip, there, other] = at_one(k, flip, there, 1 - first, other).astype(bf16)
            elif stage == 1:
                scatters[k][0, b, flip].wait_recv()
                to_two[k][flip, there] = at_two(k, flip, there, first, 1 - second).astype(bf16)
            else:
                scatters[k][1, b, flip].wait_recv()
                to_z[k][b - 1, :, side[k][flip]] = at_z(k, flip, there).astype(bf16)
            if stage < 2:
                begin(scatters[k][stage, b, flip])
        if stage == 2:
            begin(scatters[k][2, b])

    def finish(k):
        if not z_last[k]:
            for b in range(1, 4):
                scatters[k][2, b].wait_recv()
        for flip in range(2):
            scatters[k][1, 0, flip].wait_recv()
            total = at_z(k, flip, z)
            if not z_last[k]:
                for b in range(1, 4):
                    total += from_z[k][b - 1, :, side[k][flip]].astype(f32)
            start = starts[k] + flip * halves[k]
            out_ref[:, start:start + halves[k]] = total.astype(bf16)

    for copy in metas_out[0:3]:
        begin(copy)
    for stage, k, at in first_sends:
        begin(gathers[k][3, at] if stage else gathers[k][0, 0, at])
    for event in order:
        kind, at = event[0], event[1:]
        if kind == META:
            meta_step(*at)
        elif kind == GATHER:
            gather_step(*at)
        elif kind == PROJECT:
            project(*at)
        elif kind == PRODUCE:
            produce(*at)
        elif kind == SCATTER:
            scatter_step(*at)
        else:
            finish(*at)

    for copy in started:
        copy.wait_send()


def fused_body(chunks, first_sends, order, tokens, expert_ids, backup_ids, scores, gate_weight, up_weight, down_weight):
    device_count = lax.axis_size(("gx", "gy"))
    tok_rows, top = expert_ids.shape
    model, ff = gate_weight.shape[1:]
    cap = tok_rows * top
    quota = max(1, cap // (4 * device_count))
    slots = cap + device_count * quota
    count = len(chunks)
    bf16, f32 = jnp.bfloat16, jnp.float32
    grid = (4, 2, 2)
    vmem = lambda shape, kind: pltpu.VMEM(shape, kind)
    pairs = lambda lead, kind: tuple(vmem(lead + (tok_rows, 2 * half), kind) for half, _ in chunks)
    each = lambda lead, kind: tuple(vmem((2,) + lead + (tok_rows, half), kind) for half, _ in chunks)
    to_planes = tuple(
        vmem(((3, 2, 2) if z_last else (3,)) + (tok_rows, 2 * half), bf16) for half, z_last in chunks)
    scratch = [
        vmem((top, tok_rows), jnp.int32), vmem((top, tok_rows), jnp.int32), vmem((top, tok_rows), f32),
        pltpu.SemaphoreType.DMA((3 + count,)),
        vmem((128, 128), f32), vmem((512, 512), bf16), vmem((512, 512), bf16), vmem(grid + (2, tok_rows, 128), f32),
        pairs(grid + (2,), bf16),
        vmem((model, ff), bf16), vmem((model, ff), bf16), tuple(vmem((ff, 2 * half), bf16) for half, _ in chunks),
        vmem((slots, 512), bf16), vmem((16, 2, tok_rows, slots), bf16),
        vmem((slots, ff), f32), vmem((slots, ff), f32), vmem((slots, ff), bf16),
        pairs(grid, f32), pairs(grid, bf16), pairs(grid, bf16),
        each((4, 2), bf16), each((4, 2), bf16), each((4,), bf16), each((4,), bf16), to_planes, to_planes,
        pltpu.SemaphoreType.DMA((7,)), pltpu.SemaphoreType.DMA((7,)),
        pltpu.SemaphoreType.DMA((count, 24)), pltpu.SemaphoreType.DMA((count, 24)),
        pltpu.SemaphoreType.DMA((count, 20)), pltpu.SemaphoreType.DMA((count, 20)),
        pltpu.SemaphoreType.DMA((3, count)),
    ]
    whole = pl.BlockSpec(memory_space=pltpu.VMEM)
    away = pl.BlockSpec(memory_space=pl.ANY)
    return pl.pallas_call(
        functools.partial(exchange, (chunks, first_sends, order, device_count, cap, quota, slots, top)),
        out_shape=pltpu.VMEM((tok_rows, model), bf16),
        in_specs=[away] * 7,
        out_specs=whole,
        scratch_shapes=scratch,
        compiler_params=pltpu.CompilerParams(
            collective_id=0, has_side_effects=True, vmem_limit_bytes=60 * 1024 * 1024),
    )(tokens, expert_ids.T, backup_ids.T, scores.T, gate_weight, up_weight, down_weight)


META, GATHER, PROJECT, PRODUCE, SCATTER, FINISH = range(6)
CHUNKS = ((768, 0), (768, 0), (256, 1))
FIRST = (
    (3, 0, 1), (0, 2, 0), (0, 2, 1), (3, 0, 2), (3, 1, 2), (0, 1, 1), (0, 0, 1), (3, 1, 1), (0, 1, 0),
    (3, 0, 3), (3, 1, 3), (0, 0, 0),
)
ORDER = (
    (GATHER, 1, 2, 0), (META, 0), (GATHER, 0, 0, 1), (GATHER, 1, 0, 0), (GATHER, 0, 0, 2), (GATHER, 1, 1, 0),
    (META, 1), (GATHER, 0, 1, 1), (GATHER, 0, 1, 2), (GATHER, 1, 0, 1), (GATHER, 2, 2, 0), (GATHER, 0, 0, 3),
    (GATHER, 1, 0, 2), (META, 2), (GATHER, 0, 1, 3), (GATHER, 1, 1, 1), (GATHER, 2, 2, 1), (GATHER, 1, 0, 3),
    (GATHER, 2, 1, 0), (GATHER, 1, 1, 3), (GATHER, 2, 0, 2), (GATHER, 2, 1, 1), (GATHER, 1, 1, 2),
    (GATHER, 2, 0, 0), (GATHER, 2, 0, 1), (GATHER, 2, 0, 3), (GATHER, 2, 2, 3), (GATHER, 2, 2, 2),
    (GATHER, 2, 1, 3), (PROJECT, 0), (GATHER, 2, 1, 2), (PROJECT, 2), (PROJECT, 1), (PRODUCE, 0), (PRODUCE, 2),
    (SCATTER, 0, 0, 3), (SCATTER, 0, 0, 1), (SCATTER, 0, 0, 2), (SCATTER, 3, 2, 0), (PRODUCE, 1),
    (SCATTER, 0, 0, 0), (SCATTER, 1, 0, 3), (SCATTER, 0, 1, 3), (SCATTER, 1, 0, 2), (SCATTER, 0, 1, 2),
    (SCATTER, 0, 1, 1), (SCATTER, 2, 0, 3), (SCATTER, 1, 1, 3), (SCATTER, 2, 0, 2), (SCATTER, 1, 0, 1),
    (SCATTER, 1, 1, 2), (SCATTER, 0, 2, 0), (SCATTER, 0, 1, 0), (SCATTER, 1, 1, 1), (SCATTER, 2, 1, 3),
    (SCATTER, 1, 0, 0), (SCATTER, 2, 0, 1), (SCATTER, 2, 1, 2), (SCATTER, 1, 1, 0), (SCATTER, 1, 2, 0),
    (SCATTER, 2, 1, 1), (FINISH, 0), (FINISH, 2), (FINISH, 1),
)


def pick_body(mesh):
    if mesh.shape["gx"] == 4 and mesh.shape["gy"] == 8:
        return functools.partial(fused_body, CHUNKS, FIRST, ORDER)
    return on_device


def solution(mesh):
    placed = (
        P(("gx", "gy"), None),
        P(("gx", "gy"), None),
        P(("gx", "gy"), None),
        P(("gx", "gy"), None),
        P(("gx", "gy"), None, None),
        P(("gx", "gy"), None, None),
        P(("gx", "gy"), None, None),
    )
    return jax.shard_map(
        pick_body(mesh), mesh=mesh, in_specs=placed, out_specs=P(("gx", "gy"), None), check_vma=False
    )
```

```python
import functools
import jax
import jax.numpy as jnp
from jax import lax
from jax.experimental import pallas as pl
from jax.experimental.pallas import tpu as pltpu
from jax.sharding import PartitionSpec as P


def earlier_total(table):
    row = lax.broadcasted_iota(jnp.int32, (table.shape[0],) * 2, 0)
    col = lax.broadcasted_iota(jnp.int32, (table.shape[0],) * 2, 1)
    lower = (col < row).astype(jnp.bfloat16)
    total = jnp.dot(lower, table.astype(jnp.bfloat16), preferred_element_type=jnp.float32)
    return total.astype(jnp.int32)


def ranks_within(numbers, active, expert_count):
    table = (
        (numbers[:, None] == jnp.arange(expert_count, dtype=jnp.int32)[None, :]) & active[:, None]
    ).astype(jnp.int32)
    within = jnp.sum(earlier_total(table) * table, axis=1)
    return (within, table)


def pack_rows(tokens, destination, active, slot_total, top_count):
    pick_number = jnp.arange(destination.shape[0], dtype=jnp.int32)
    match_grid = (
        destination[None, :] == jnp.arange(slot_total, dtype=jnp.int32)[:, None]
    ) & active[None, :]
    source = jnp.sum(jnp.where(match_grid, pick_number[None, :] + 1, 0), axis=1) - 1
    picked_rows = jnp.take(tokens, jnp.maximum(source, 0) // top_count, axis=0)
    return jnp.where((source >= 0)[:, None], picked_rows, jnp.zeros((), tokens.dtype))


def send_rows(slot_rows):
    return lax.all_to_all(slot_rows, ("gx", "gy"), split_axis=0, concat_axis=0, tiled=True)


def on_device(tokens, expert_ids, backup_ids, scores, gate_weight, up_weight, down_weight):
    device_count = lax.axis_size(("gx", "gy"))
    own_index = lax.axis_index(("gx", "gy"))
    tok_rows, top_count = expert_ids.shape
    model_width = tokens.shape[1]
    per_source = tok_rows * top_count
    spare_quota = max(1, per_source // (4 * device_count))
    most_rows = max(2, (3 * per_source + 2 * device_count - 1) // (2 * device_count))
    first_flat = expert_ids.reshape(-1)
    backup_flat = backup_ids.reshape(-1)
    everyone = jnp.ones((per_source,), dtype=bool)
    first_within, first_table = ranks_within(first_flat, everyone, device_count)
    own_counts = jnp.sum(first_table, axis=0)
    all_counts = lax.all_gather(own_counts[None, :], ("gx", "gy"), axis=0, tiled=True)
    before = earlier_total(all_counts)
    own_before = lax.dynamic_index_in_dim(before, own_index, 0, keepdims=False)
    first_rank = jnp.sum(first_table * own_before[None, :], axis=1) + first_within
    kept_mask = first_rank < per_source
    spilled = jnp.logical_not(kept_mask)
    spill_rank = ranks_within(backup_flat, spilled, device_count)[0]
    spare_mask = spilled & (spill_rank < spare_quota)
    send_first = pack_rows(
        tokens,
        first_flat * most_rows + first_within,
        kept_mask,
        device_count * most_rows,
        top_count,
    ).reshape(device_count, most_rows, model_width)
    send_spill = pack_rows(
        tokens,
        backup_flat * spare_quota + spill_rank,
        spare_mask,
        device_count * spare_quota,
        top_count,
    ).reshape(device_count, spare_quota, model_width)
    recv_first = send_rows(send_first)
    recv_spill = send_rows(send_spill)
    count_column = lax.dynamic_index_in_dim(all_counts, own_index, 1, keepdims=False)
    before_column = lax.dynamic_index_in_dim(before, own_index, 1, keepdims=False)
    ending = before_column + count_column
    row_number = jnp.arange(per_source, dtype=jnp.int32)
    source_of_row = jnp.sum((ending[None, :] <= row_number[:, None]).astype(jnp.int32), axis=1)
    owner_grid = source_of_row[:, None] == jnp.arange(device_count, dtype=jnp.int32)[None, :]
    start_of_row = jnp.sum(jnp.where(owner_grid, before_column[None, :], 0), axis=1)
    filled = row_number < ending[device_count - 1]
    slot_index = jnp.minimum(source_of_row, device_count - 1) * most_rows + jnp.clip(
        row_number - start_of_row, 0, most_rows - 1
    )
    first_rows = jnp.take(
        recv_first.reshape(device_count * most_rows, model_width), slot_index, axis=0
    )
    first_rows = jnp.where(filled[:, None], first_rows, jnp.zeros((), first_rows.dtype))
    expert_rows = jnp.concatenate(
        [first_rows, recv_spill.reshape(device_count * spare_quota, model_width)], axis=0
    )
    gate = jnp.dot(expert_rows, gate_weight[0], preferred_element_type=jnp.float32)
    upward = jnp.dot(expert_rows, up_weight[0], preferred_element_type=jnp.float32)
    hidden = (jax.nn.silu(gate) * upward).astype(jnp.bfloat16)
    expert_out = jnp.dot(hidden, down_weight[0], preferred_element_type=jnp.float32).astype(
        jnp.bfloat16
    )
    position = jnp.arange(most_rows, dtype=jnp.int32)
    rank_grid = before_column[:, None] + position[None, :]
    live_slot = (position[None, :] < count_column[:, None]) & (rank_grid < per_source)
    back_first = jnp.take(expert_out[:per_source], jnp.clip(rank_grid, 0, per_source - 1), axis=0)
    back_first = jnp.where(live_slot[:, :, None], back_first, jnp.zeros((), back_first.dtype))
    back_spill = expert_out[per_source:].reshape(device_count, spare_quota, model_width)
    home_first = send_rows(back_first)
    home_spill = send_rows(back_spill)
    first_slot = jnp.minimum(first_flat * most_rows + first_within, device_count * most_rows - 1)
    spill_slot = backup_flat * spare_quota + jnp.minimum(spill_rank, spare_quota - 1)
    picked_first = jnp.take(
        home_first.reshape(device_count * most_rows, model_width), first_slot, axis=0
    )
    picked_spill = jnp.take(
        home_spill.reshape(device_count * spare_quota, model_width), spill_slot, axis=0
    )
    picked = jnp.where(kept_mask[:, None], picked_first, picked_spill).reshape(
        tok_rows, top_count, model_width
    )
    route_weights = scores / jnp.sum(scores, axis=1, keepdims=True)
    weights = jnp.where(
        (kept_mask | spare_mask).reshape(tok_rows, top_count),
        route_weights,
        jnp.zeros((), jnp.float32),
    )
    mixed = jnp.sum(weights[:, :, None] * picked.astype(jnp.float32), axis=1)
    return mixed.astype(jnp.bfloat16)


def exchange(cfg, tok_hbm, ids_hbm, backups_hbm, scores_hbm, gate_hbm, up_hbm, down_hbm, out_ref,
             ids_ref, backups_ref, scores_ref, in_sem, flipped, before, near, metas, toks, wg, wu, wd, pick, comb, gate, upward, hidden,
             own, to_core, from_core, to_one, from_one, to_two, from_two, to_z, from_z, to_plane, from_plane,
             meta_send, meta_recv, ag_send, ag_recv, rs_send, rs_recv, w_sem):
    chunks, first_sends, order, experts, cap, quota, slots, top = cfg
    halves = [chunk[0] for chunk in chunks]
    late = [chunk[1] for chunk in chunks]
    count = len(chunks)
    starts = [2 * sum(halves[:k]) for k in range(count)]
    columns = [pl.ds(starts[k], 2 * halves[k]) for k in range(count)]
    side = [[pl.ds(0, half), pl.ds(half, half)] for half in halves]
    bf16, f32 = jnp.bfloat16, jnp.float32
    z = lax.axis_index("gx")
    g = lax.axis_index("gy")
    c = lax.rem(g, 2)
    x = lax.rem(lax.div(g, 2), 2)
    y = lax.div(g, 4)
    core_peer = (z, g + 1 - 2 * c)
    x_peer = (z, g + 2 - 4 * x)
    y_peer = (z, g + 4 - 8 * y)
    far_peer = (z, 6 - 4 * y - 2 * x + c)
    planes = [z, z + 1 - 2 * lax.rem(z, 2), z + 2 - 4 * lax.div(z, 2), 3 - z]
    z_peers = [(there, g) for there in planes[1:]]
    expert = z * 8 + g

    def remote(src, dst, send, recv, device):
        return pltpu.make_async_remote_copy(
            src_ref=src, dst_ref=dst, send_sem=send, recv_sem=recv,
            device_id=device, device_id_type=pl.DeviceIdType.MESH)

    barrier = pltpu.get_barrier_semaphore()
    for peer in [core_peer, x_peer, y_peer, far_peer] + z_peers:
        pl.semaphore_signal(barrier, inc=1, device_id=peer, device_id_type=pl.DeviceIdType.MESH)

    small_copies = [pltpu.make_async_copy(src, dst, in_sem.at[i]) for i, (src, dst) in enumerate(
        ((ids_hbm, ids_ref), (backups_hbm, backups_ref), (scores_hbm, scores_ref)))]
    token_copies = [pltpu.make_async_copy(tok_hbm.at[:, columns[k]], toks[k].at[z, y, x, c], in_sem.at[3 + k])
                    for k in range(count)]
    for copy in small_copies + token_copies:
        copy.start()
    for copy in small_copies + token_copies:
        copy.wait()
    weight_copies = []
    for k in range(count):
        pair = [pltpu.make_async_copy(gate_hbm.at[0, columns[k]], wg.at[columns[k]], w_sem.at[0, k]),
                pltpu.make_async_copy(up_hbm.at[0, columns[k]], wu.at[columns[k]], w_sem.at[1, k])]
        weight_copies.append(pair)
        for copy in pair:
            copy.start()
    down_copies = []
    for k in range(count):
        copy = pltpu.make_async_copy(down_hbm.at[0, :, columns[k]], wd[k], w_sem.at[2, k])
        copy.start()
        down_copies.append(copy)

    scores = scores_ref[...]
    flipped[0:3 * top, 0:16] = jnp.concatenate(
        [ids_ref[...].astype(f32), backups_ref[...].astype(f32),
         scores / jnp.sum(scores, axis=0, keepdims=True)], axis=0)
    metas[z, y, x, c] = flipped[...].T[0:16].astype(bf16)
    row = lax.broadcasted_iota(jnp.int32, (512, 512), 0)
    col = lax.broadcasted_iota(jnp.int32, (512, 512), 1)
    before[...] = jnp.where(row < col, 1.0, 0.0).astype(bf16)
    same = lax.shift_right_logical(row, 4) == lax.shift_right_logical(col, 4)
    near[...] = jnp.where(same & (row < col), 1.0, 0.0).astype(bf16)
    pl.semaphore_wait(barrier, 7)

    started = []

    def begin(copy):
        copy.start()
        started.append(copy)

    meta_parts = [metas.at[z, y, x, c]] * 3 + [metas.at[:, y, x, c]] * 3 + [metas.at[:, :, :, c]]
    meta_peers = z_peers + [x_peer, y_peer, far_peer, core_peer]
    metas_out = [remote(meta_parts[i], meta_parts[i], meta_send.at[i], meta_recv.at[i], meta_peers[i])
                 for i in range(7)]

    def gather_copies(k):
        buf, table = toks[k], {}
        sem = lambda at: (ag_send.at[k, at], ag_recv.at[k, at])
        for b, there in enumerate(planes):
            whole = buf.at[there, :, :, c]
            for flip in range(2):
                line = buf.at[there, y, x, c, :, side[k][flip]]
                plane = (buf.at[there, :, x, c, :, side[k][1]] if flip else buf.at[there, y, :, c, :, side[k][0]])
                one, two = (y_peer, x_peer) if flip else (x_peer, y_peer)
                if b not in late[k]:
                    table[0, b, flip] = remote(line, line, *sem(6 * b + flip), one)
                    table[1, b, flip] = remote(plane, plane, *sem(6 * b + 2 + flip), two)
            table[2, b] = remote(whole, whole, *sem(6 * b + 4), core_peer)
            if b:
                mine = buf.at[z, :, :, c] if b in late[k] else buf.at[z, y, x, c]
                table[3, b] = remote(mine, mine, *sem(6 * b + 5), z_peers[b - 1])
        return table

    gathers = [gather_copies(k) for k in range(count)]

    def route():
        record = metas[...].reshape(512, 128).astype(f32).T
        first, backup, weight = record[0:top], record[top:2 * top], record[2 * top:3 * top]
        number = lax.broadcasted_iota(jnp.int32, (experts, 512), 0).astype(f32)
        named = jnp.zeros((experts, 512), f32)
        for k in range(top):
            named += jnp.where(first[k:k + 1] == number, 1.0, 0.0)
        rank = jnp.dot(named.astype(bf16), before[...], preferred_element_type=f32)
        spilled = jnp.where(rank >= cap, named, 0.0)
        me = expert.astype(f32)
        is_me = jnp.where(number == me, 1.0, 0.0)
        total = lambda table: jnp.sum(table, axis=0, keepdims=True)
        my_named = total(is_me * named)
        my_rank = total(is_me * rank)
        my_weight = total(jnp.where(first == me, weight, 0.0))
        has_backup = total(jnp.where(backup == me, 1.0, 0.0))
        its_first = total(jnp.where(backup == me, first, 0.0))
        its_weight = total(jnp.where(backup == me, weight, 0.0))
        moved = has_backup * total(jnp.where(number == its_first, spilled, 0.0))
        moved_wide = jnp.broadcast_to(moved, (16, 512))
        spill_rank = jnp.dot(moved_wide.astype(bf16), near[...], preferred_element_type=f32)[0:1]
        token = lax.broadcasted_iota(jnp.int32, (1, 512), 1)
        block = lax.shift_right_logical(token, 4).astype(f32)
        kept_slot = lax.broadcasted_iota(jnp.int32, (cap, 512), 0).astype(f32)
        spare_slot = lax.broadcasted_iota(jnp.int32, (slots - cap, 512), 0).astype(f32)
        spare_at = jnp.where(spill_rank < quota, block * quota + spill_rank, -1.0)
        kept_grid = jnp.where(my_rank == kept_slot, my_named, 0.0)
        spare_grid = jnp.where(spare_at == spare_slot, moved, 0.0)
        pick[...] = jnp.concatenate([kept_grid, spare_grid], axis=0).astype(bf16)
        mixing = jnp.concatenate([kept_grid * my_weight, spare_grid * its_weight], axis=0)
        comb[...] = mixing.T.astype(bf16).reshape(16, 2, 16, slots)

    def meta_step(i):
        waits, sends = ((range(0, 3), range(3, 6)), (range(3, 6), range(6, 7)), (range(6, 7), ()))[i]
        for at in waits:
            metas_out[at].wait_recv()
        for at in sends:
            begin(metas_out[at])
        if i == 2:
            route()

    def gather_step(stage, k, b):
        if b in late[k] or stage == 0:
            gathers[k][3, b].wait_recv()
        else:
            for flip in range(2):
                gathers[k][stage - 1, b, flip].wait_recv()
        if stage < 2:
            for flip in range(2):
                begin(gathers[k][stage, b, flip])
            return
        if b == 0:
            for other in late[k]:
                begin(gathers[k][3, other])
        begin(gathers[k][2, b])

    projected = []

    def project(k):
        for b in range(4):
            gathers[k][2, b].wait_recv()
        for copy in weight_copies[k]:
            copy.wait()
        rows = jnp.dot(pick[...], toks[k][...].reshape(512, 2 * halves[k]), preferred_element_type=f32).astype(bf16)
        new_gate = jnp.dot(rows, wg[columns[k], :], preferred_element_type=f32)
        new_up = jnp.dot(rows, wu[columns[k], :], preferred_element_type=f32)
        projected.append(k)
        if len(projected) == 1:
            gate[...] = new_gate
            upward[...] = new_up
        elif len(projected) < count:
            gate[...] += new_gate
            upward[...] += new_up
        else:
            full = gate[...] + new_gate
            hidden[...] = (full / (1.0 + jnp.exp(-full)) * (upward[...] + new_up)).astype(bf16)

    def scatter_copies(k):
        table = {}
        sem = lambda at: (rs_send.at[k, at], rs_recv.at[k, at])
        for b, there in enumerate(planes):
            for flip in range(2):
                one, two = (x_peer, y_peer) if flip else (y_peer, x_peer)
                if b not in late[k]:
                    table[0, b, flip] = remote(to_one[k].at[flip, there], from_one[k].at[flip, there],
                                               *sem(5 * b + flip), one)
                    table[1, b, flip] = remote(to_two[k].at[flip, there], from_two[k].at[flip, there],
                                               *sem(5 * b + 2 + flip), two)
            if b in late[k]:
                at = late[k].index(b)
                table[2, b] = remote(to_plane[k].at[at], from_plane[k].at[at], *sem(5 * b + 4), z_peers[b - 1])
            elif b:
                table[2, b] = remote(to_z[k].at[b - 1], from_z[k].at[b - 1], *sem(5 * b + 4), z_peers[b - 1])
        return table

    cores = [remote(to_core[k], from_core[k], rs_send.at[k, 4], rs_recv.at[k, 4], core_peer) for k in range(count)]
    scatters = [scatter_copies(k) for k in range(count)]

    def produce(k):
        down_copies[k].wait()
        rows = jnp.dot(hidden[...], wd[k][...], preferred_element_type=f32).astype(bf16)
        sides = jnp.concatenate([comb[:, 1 - c].reshape(256, slots), comb[:, c].reshape(256, slots)], axis=0)
        mixed = jnp.dot(sides, rows, preferred_element_type=f32)
        to_core[k][...] = mixed[:256].astype(bf16).reshape(4, 2, 2, 16, 2 * halves[k])
        begin(cores[k])
        own[k][...] = mixed[256:].reshape(4, 2, 2, 16, 2 * halves[k])

    def at_one(k, flip, b, first, second):
        yy, xx = (second, first) if flip else (first, second)
        mine = own[k][planes[b], yy, xx, :, side[k][flip]]
        if late[k] and b == 0:
            return mine
        return mine + from_core[k][planes[b], yy, xx, :, side[k][flip]].astype(f32)

    def at_two(k, flip, b, first, second):
        return at_one(k, flip, b, first, second) + from_one[k][flip, planes[b], second].astype(f32)

    def at_z(k, flip, b):
        first, second = (x, y) if flip else (y, x)
        return at_two(k, flip, b, first, second) + from_two[k][flip, planes[b]].astype(f32)

    joined = []

    def scatter_step(stage, k, b):
        there = planes[b]
        if k not in joined:
            joined.append(k)
            cores[k].wait_recv()
        if stage == 3:
            for at, other in reversed(list(enumerate(late[k]))):
                total = own[k][planes[other]] + from_core[k][planes[other]].astype(f32)
                to_plane[k][at] = total.astype(bf16)
                begin(scatters[k][2, other])
            return
        if stage == 0 and late[k] and b == 0:
            total = own[k][z] + from_core[k][z].astype(f32)
            for at, other in enumerate(late[k]):
                scatters[k][2, other].wait_recv()
                total += from_plane[k][at].astype(f32)
            own[k][z] = total
        for flip in range(2):
            first, second = (x, y) if flip else (y, x)
            if stage == 0:
                for other in range(2):
                    to_one[k][flip, there, other] = at_one(k, flip, b, 1 - first, other).astype(bf16)
            elif stage == 1:
                scatters[k][0, b, flip].wait_recv()
                to_two[k][flip, there] = at_two(k, flip, b, first, 1 - second).astype(bf16)
            else:
                scatters[k][1, b, flip].wait_recv()
                to_z[k][b - 1, :, side[k][flip]] = at_z(k, flip, b).astype(bf16)
            if stage < 2:
                begin(scatters[k][stage, b, flip])
        if stage == 2:
            begin(scatters[k][2, b])

    def finish(k):
        early = [b for b in range(1, 4) if b not in late[k]]
        for b in early:
            scatters[k][2, b].wait_recv()
        for flip in range(2):
            scatters[k][1, 0, flip].wait_recv()
            total = at_z(k, flip, 0)
            for b in early:
                total += from_z[k][b - 1, :, side[k][flip]].astype(f32)
            start = starts[k] + flip * halves[k]
            out_ref[:, start:start + halves[k]] = total.astype(bf16)

    for copy in metas_out[0:3]:
        begin(copy)
    for stage, k, at in first_sends:
        begin(gathers[k][3, at] if stage else gathers[k][0, 0, at])
    for event in order:
        kind, at = event[0], event[1:]
        if kind == META:
            meta_step(*at)
        elif kind == GATHER:
            gather_step(*at)
        elif kind == PROJECT:
            project(*at)
        elif kind == PRODUCE:
            produce(*at)
        elif kind == SCATTER:
            scatter_step(*at)
        else:
            finish(*at)

    for copy in started:
        copy.wait_send()


def fused_body(chunks, first_sends, order, tokens, expert_ids, backup_ids, scores, gate_weight, up_weight, down_weight):
    device_count = lax.axis_size(("gx", "gy"))
    tok_rows, top = expert_ids.shape
    model, ff = gate_weight.shape[1:]
    cap = tok_rows * top
    quota = max(1, cap // (4 * device_count))
    slots = cap + device_count * quota
    count = len(chunks)
    bf16, f32 = jnp.bfloat16, jnp.float32
    grid = (4, 2, 2)
    vmem = lambda shape, kind: pltpu.VMEM(shape, kind)
    pairs = lambda lead, kind: tuple(vmem(lead + (tok_rows, 2 * half), kind) for half, _ in chunks)
    each = lambda lead, kind: tuple(vmem((2,) + lead + (tok_rows, half), kind) for half, _ in chunks)
    lines = pairs((3,), bf16)
    to_planes = tuple(vmem((max(1, len(late)), 2, 2, tok_rows, 2 * half), bf16) for half, late in chunks)
    scratch = [
        vmem((top, tok_rows), jnp.int32), vmem((top, tok_rows), jnp.int32), vmem((top, tok_rows), f32),
        pltpu.SemaphoreType.DMA((3 + count,)),
        vmem((128, 128), f32), vmem((512, 512), bf16), vmem((512, 512), bf16), vmem(grid + (2, tok_rows, 128), bf16),
        pairs(grid + (2,), bf16),
        vmem((model, ff), bf16), vmem((model, ff), bf16), tuple(vmem((ff, 2 * half), bf16) for half, _ in chunks),
        vmem((slots, 512), bf16), vmem((16, 2, tok_rows, slots), bf16),
        vmem((slots, ff), f32), vmem((slots, ff), f32), vmem((slots, ff), bf16),
        pairs(grid, f32), pairs(grid, bf16), pairs(grid, bf16),
        each((4, 2), bf16), each((4, 2), bf16), each((4,), bf16), each((4,), bf16), lines, lines, to_planes, to_planes,
        pltpu.SemaphoreType.DMA((7,)), pltpu.SemaphoreType.DMA((7,)),
        pltpu.SemaphoreType.DMA((count, 24)), pltpu.SemaphoreType.DMA((count, 24)),
        pltpu.SemaphoreType.DMA((count, 20)), pltpu.SemaphoreType.DMA((count, 20)),
        pltpu.SemaphoreType.DMA((3, count)),
    ]
    whole = pl.BlockSpec(memory_space=pltpu.VMEM)
    away = pl.BlockSpec(memory_space=pl.ANY)
    return pl.pallas_call(
        functools.partial(exchange, (chunks, first_sends, order, device_count, cap, quota, slots, top)),
        out_shape=pltpu.VMEM((tok_rows, model), bf16),
        in_specs=[away] * 7,
        out_specs=whole,
        scratch_shapes=scratch,
        compiler_params=pltpu.CompilerParams(
            collective_id=0, has_side_effects=True, vmem_limit_bytes=60 * 1024 * 1024),
    )(tokens, expert_ids.T, backup_ids.T, scores.T, gate_weight, up_weight, down_weight)


META, GATHER, PROJECT, PRODUCE, SCATTER, FINISH = range(6)
CHUNKS = ((896, ()), (640, ()), (256, (1, 2, 3)))
FIRST = (
    (3, 0, 3), (0, 0, 0), (3, 0, 1), (0, 0, 1), (0, 2, 1), (3, 0, 2), (0, 2, 0), (3, 1, 1), (3, 1, 2),
    (0, 1, 0), (0, 1, 1), (3, 1, 3),
)
ORDER = (
    (GATHER, 1, 0, 0), (GATHER, 1, 2, 0), (META, 0), (GATHER, 0, 0, 1), (GATHER, 1, 1, 0), (GATHER, 0, 0, 2),
    (GATHER, 0, 0, 3), (GATHER, 0, 1, 1), (GATHER, 2, 2, 0), (GATHER, 1, 0, 1), (GATHER, 1, 0, 2),
    (GATHER, 0, 1, 2), (GATHER, 1, 0, 3), (GATHER, 0, 1, 3), (META, 1), (GATHER, 1, 1, 1), (GATHER, 2, 2, 1),
    (META, 2), (GATHER, 2, 0, 0), (GATHER, 1, 1, 2), (GATHER, 2, 1, 0), (GATHER, 2, 0, 2), (GATHER, 2, 0, 1),
    (GATHER, 2, 2, 2), (GATHER, 2, 0, 3), (GATHER, 1, 1, 3), (GATHER, 2, 2, 3), (GATHER, 2, 1, 1), (PROJECT, 0),
    (GATHER, 2, 1, 2), (GATHER, 2, 1, 3), (PROJECT, 2), (PROJECT, 1), (PRODUCE, 0), (PRODUCE, 1),
    (SCATTER, 0, 0, 3), (PRODUCE, 2), (SCATTER, 0, 0, 1), (SCATTER, 0, 0, 2), (SCATTER, 0, 1, 2),
    (SCATTER, 3, 2, 0), (SCATTER, 1, 0, 3), (SCATTER, 0, 1, 3), (SCATTER, 1, 0, 2), (SCATTER, 0, 1, 1),
    (SCATTER, 1, 0, 1), (SCATTER, 1, 1, 2), (SCATTER, 2, 0, 3), (SCATTER, 1, 1, 3), (SCATTER, 1, 1, 1),
    (SCATTER, 0, 1, 0), (SCATTER, 2, 0, 2), (SCATTER, 0, 0, 0), (SCATTER, 2, 0, 1), (SCATTER, 0, 2, 0),
    (SCATTER, 2, 1, 3), (SCATTER, 2, 1, 1), (SCATTER, 1, 1, 0), (SCATTER, 2, 1, 2), (SCATTER, 1, 0, 0),
    (SCATTER, 1, 2, 0), (FINISH, 0), (FINISH, 2), (FINISH, 1),
)


def pick_body(mesh):
    if mesh.shape["gx"] == 4 and mesh.shape["gy"] == 8:
        return functools.partial(fused_body, CHUNKS, FIRST, ORDER)
    return on_device


def solution(mesh):
    placed = (
        P(("gx", "gy"), None),
        P(("gx", "gy"), None),
        P(("gx", "gy"), None),
        P(("gx", "gy"), None),
        P(("gx", "gy"), None, None),
        P(("gx", "gy"), None, None),
        P(("gx", "gy"), None, None),
    )
    return jax.shard_map(
        pick_body(mesh), mesh=mesh, in_specs=placed, out_specs=P(("gx", "gy"), None), check_vma=False
    )
```

```python
import functools
import jax
import jax.numpy as jnp
from jax import lax
from jax.experimental import pallas as pl
from jax.experimental.pallas import tpu as pltpu
from jax.sharding import PartitionSpec as P


def earlier_total(table):
    row = lax.broadcasted_iota(jnp.int32, (table.shape[0],) * 2, 0)
    col = lax.broadcasted_iota(jnp.int32, (table.shape[0],) * 2, 1)
    lower = (col < row).astype(jnp.bfloat16)
    total = jnp.dot(lower, table.astype(jnp.bfloat16), preferred_element_type=jnp.float32)
    return total.astype(jnp.int32)


def ranks_within(numbers, active, expert_count):
    table = (
        (numbers[:, None] == jnp.arange(expert_count, dtype=jnp.int32)[None, :]) & active[:, None]
    ).astype(jnp.int32)
    within = jnp.sum(earlier_total(table) * table, axis=1)
    return (within, table)


def pack_rows(tokens, destination, active, slot_total, top_count):
    pick_number = jnp.arange(destination.shape[0], dtype=jnp.int32)
    match_grid = (
        destination[None, :] == jnp.arange(slot_total, dtype=jnp.int32)[:, None]
    ) & active[None, :]
    source = jnp.sum(jnp.where(match_grid, pick_number[None, :] + 1, 0), axis=1) - 1
    picked_rows = jnp.take(tokens, jnp.maximum(source, 0) // top_count, axis=0)
    return jnp.where((source >= 0)[:, None], picked_rows, jnp.zeros((), tokens.dtype))


def send_rows(slot_rows):
    return lax.all_to_all(slot_rows, ("gx", "gy"), split_axis=0, concat_axis=0, tiled=True)


def on_device(tokens, expert_ids, backup_ids, scores, gate_weight, up_weight, down_weight):
    device_count = lax.axis_size(("gx", "gy"))
    own_index = lax.axis_index(("gx", "gy"))
    tok_rows, top_count = expert_ids.shape
    model_width = tokens.shape[1]
    per_source = tok_rows * top_count
    spare_quota = max(1, per_source // (4 * device_count))
    most_rows = max(2, (3 * per_source + 2 * device_count - 1) // (2 * device_count))
    first_flat = expert_ids.reshape(-1)
    backup_flat = backup_ids.reshape(-1)
    everyone = jnp.ones((per_source,), dtype=bool)
    first_within, first_table = ranks_within(first_flat, everyone, device_count)
    own_counts = jnp.sum(first_table, axis=0)
    all_counts = lax.all_gather(own_counts[None, :], ("gx", "gy"), axis=0, tiled=True)
    before = earlier_total(all_counts)
    own_before = lax.dynamic_index_in_dim(before, own_index, 0, keepdims=False)
    first_rank = jnp.sum(first_table * own_before[None, :], axis=1) + first_within
    kept_mask = first_rank < per_source
    spilled = jnp.logical_not(kept_mask)
    spill_rank = ranks_within(backup_flat, spilled, device_count)[0]
    spare_mask = spilled & (spill_rank < spare_quota)
    send_first = pack_rows(
        tokens,
        first_flat * most_rows + first_within,
        kept_mask,
        device_count * most_rows,
        top_count,
    ).reshape(device_count, most_rows, model_width)
    send_spill = pack_rows(
        tokens,
        backup_flat * spare_quota + spill_rank,
        spare_mask,
        device_count * spare_quota,
        top_count,
    ).reshape(device_count, spare_quota, model_width)
    recv_first = send_rows(send_first)
    recv_spill = send_rows(send_spill)
    count_column = lax.dynamic_index_in_dim(all_counts, own_index, 1, keepdims=False)
    before_column = lax.dynamic_index_in_dim(before, own_index, 1, keepdims=False)
    ending = before_column + count_column
    row_number = jnp.arange(per_source, dtype=jnp.int32)
    source_of_row = jnp.sum((ending[None, :] <= row_number[:, None]).astype(jnp.int32), axis=1)
    owner_grid = source_of_row[:, None] == jnp.arange(device_count, dtype=jnp.int32)[None, :]
    start_of_row = jnp.sum(jnp.where(owner_grid, before_column[None, :], 0), axis=1)
    filled = row_number < ending[device_count - 1]
    slot_index = jnp.minimum(source_of_row, device_count - 1) * most_rows + jnp.clip(
        row_number - start_of_row, 0, most_rows - 1
    )
    first_rows = jnp.take(
        recv_first.reshape(device_count * most_rows, model_width), slot_index, axis=0
    )
    first_rows = jnp.where(filled[:, None], first_rows, jnp.zeros((), first_rows.dtype))
    expert_rows = jnp.concatenate(
        [first_rows, recv_spill.reshape(device_count * spare_quota, model_width)], axis=0
    )
    gate = jnp.dot(expert_rows, gate_weight[0], preferred_element_type=jnp.float32)
    upward = jnp.dot(expert_rows, up_weight[0], preferred_element_type=jnp.float32)
    hidden = (jax.nn.silu(gate) * upward).astype(jnp.bfloat16)
    expert_out = jnp.dot(hidden, down_weight[0], preferred_element_type=jnp.float32).astype(
        jnp.bfloat16
    )
    position = jnp.arange(most_rows, dtype=jnp.int32)
    rank_grid = before_column[:, None] + position[None, :]
    live_slot = (position[None, :] < count_column[:, None]) & (rank_grid < per_source)
    back_first = jnp.take(expert_out[:per_source], jnp.clip(rank_grid, 0, per_source - 1), axis=0)
    back_first = jnp.where(live_slot[:, :, None], back_first, jnp.zeros((), back_first.dtype))
    back_spill = expert_out[per_source:].reshape(device_count, spare_quota, model_width)
    home_first = send_rows(back_first)
    home_spill = send_rows(back_spill)
    first_slot = jnp.minimum(first_flat * most_rows + first_within, device_count * most_rows - 1)
    spill_slot = backup_flat * spare_quota + jnp.minimum(spill_rank, spare_quota - 1)
    picked_first = jnp.take(
        home_first.reshape(device_count * most_rows, model_width), first_slot, axis=0
    )
    picked_spill = jnp.take(
        home_spill.reshape(device_count * spare_quota, model_width), spill_slot, axis=0
    )
    picked = jnp.where(kept_mask[:, None], picked_first, picked_spill).reshape(
        tok_rows, top_count, model_width
    )
    route_weights = scores / jnp.sum(scores, axis=1, keepdims=True)
    weights = jnp.where(
        (kept_mask | spare_mask).reshape(tok_rows, top_count),
        route_weights,
        jnp.zeros((), jnp.float32),
    )
    mixed = jnp.sum(weights[:, :, None] * picked.astype(jnp.float32), axis=1)
    return mixed.astype(jnp.bfloat16)


def exchange(cfg, tok_hbm, ids_hbm, backups_hbm, scores_hbm, gate_hbm, up_hbm, down_hbm, out_ref,
             ids_ref, backups_ref, scores_ref, in_sem, flipped, before, near, metas, toks, wg, wu, wd, pick, comb, gate, upward, hidden,
             own, to_core, from_core, to_one, from_one, to_two, from_two, to_z, from_z, to_plane, from_plane,
             meta_send, meta_recv, ag_send, ag_recv, rs_send, rs_recv, w_sem):
    chunks, first_sends, order, experts, cap, quota, slots, top = cfg
    halves = [chunk[0] for chunk in chunks]
    late = [chunk[1] for chunk in chunks]
    count = len(chunks)
    starts = [2 * sum(halves[:k]) for k in range(count)]
    columns = [pl.ds(starts[k], 2 * halves[k]) for k in range(count)]
    side = [[pl.ds(0, half), pl.ds(half, half)] for half in halves]
    bf16, f32 = jnp.bfloat16, jnp.float32
    z = lax.axis_index("gx")
    g = lax.axis_index("gy")
    c = lax.rem(g, 2)
    x = lax.rem(lax.div(g, 2), 2)
    y = lax.div(g, 4)
    core_peer = (z, g + 1 - 2 * c)
    x_peer = (z, g + 2 - 4 * x)
    y_peer = (z, g + 4 - 8 * y)
    far_peer = (z, 6 - 4 * y - 2 * x + c)
    planes = [z, z + 1 - 2 * lax.rem(z, 2), z + 2 - 4 * lax.div(z, 2), 3 - z]
    z_peers = [(there, g) for there in planes[1:]]
    expert = z * 8 + g

    def remote(src, dst, send, recv, device):
        return pltpu.make_async_remote_copy(
            src_ref=src, dst_ref=dst, send_sem=send, recv_sem=recv,
            device_id=device, device_id_type=pl.DeviceIdType.MESH)

    barrier = pltpu.get_barrier_semaphore()
    for peer in [core_peer, x_peer, y_peer, far_peer] + z_peers:
        pl.semaphore_signal(barrier, inc=1, device_id=peer, device_id_type=pl.DeviceIdType.MESH)

    small_copies = [pltpu.make_async_copy(src, dst, in_sem.at[i]) for i, (src, dst) in enumerate(
        ((ids_hbm, ids_ref), (backups_hbm, backups_ref), (scores_hbm, scores_ref)))]
    token_copies = [pltpu.make_async_copy(tok_hbm.at[:, columns[k]], toks[k].at[z, y, x, c], in_sem.at[3 + k])
                    for k in range(count)]
    for copy in small_copies + token_copies:
        copy.start()
    for copy in small_copies:
        copy.wait()
    scores = scores_ref[...]
    flipped[0:3 * top, 0:16] = jnp.concatenate(
        [ids_ref[...].astype(f32), backups_ref[...].astype(f32),
         scores / jnp.sum(scores, axis=0, keepdims=True)], axis=0)
    metas[z, y, x, c] = flipped[...].T[0:16].astype(bf16)
    for copy in token_copies:
        copy.wait()
    pl.semaphore_wait(barrier, 7)

    started = []

    def begin(copy):
        copy.start()
        started.append(copy)

    meta_parts = [metas.at[z, y, x, c]] * 3 + [metas.at[:, y, x, c]] * 3 + [metas.at[:, :, :, c]]
    meta_peers = z_peers + [x_peer, y_peer, far_peer, core_peer]
    metas_out = [remote(meta_parts[i], meta_parts[i], meta_send.at[i], meta_recv.at[i], meta_peers[i])
                 for i in range(7)]

    def gather_copies(k):
        buf, table = toks[k], {}
        sem = lambda at: (ag_send.at[k, at], ag_recv.at[k, at])
        for b, there in enumerate(planes):
            whole = buf.at[there, :, :, c]
            for flip in range(2):
                line = buf.at[there, y, x, c, :, side[k][flip]]
                plane = (buf.at[there, :, x, c, :, side[k][1]] if flip else buf.at[there, y, :, c, :, side[k][0]])
                one, two = (y_peer, x_peer) if flip else (x_peer, y_peer)
                if b not in late[k]:
                    table[0, b, flip] = remote(line, line, *sem(6 * b + flip), one)
                    table[1, b, flip] = remote(plane, plane, *sem(6 * b + 2 + flip), two)
            table[2, b] = remote(whole, whole, *sem(6 * b + 4), core_peer)
            if b:
                mine = buf.at[z, :, :, c] if b in late[k] else buf.at[z, y, x, c]
                table[3, b] = remote(mine, mine, *sem(6 * b + 5), z_peers[b - 1])
        return table

    gathers = [gather_copies(k) for k in range(count)]

    def route():
        record = metas[...].reshape(512, 128).astype(f32).T
        first, backup, weight = record[0:top], record[top:2 * top], record[2 * top:3 * top]
        number = lax.broadcasted_iota(jnp.int32, (experts, 512), 0).astype(f32)
        named = jnp.zeros((experts, 512), f32)
        for k in range(top):
            named += jnp.where(first[k:k + 1] == number, 1.0, 0.0)
        rank = jnp.dot(named.astype(bf16), before[...], preferred_element_type=f32)
        spilled = jnp.where(rank >= cap, named, 0.0)
        me = expert.astype(f32)
        is_me = jnp.where(number == me, 1.0, 0.0)
        total = lambda table: jnp.sum(table, axis=0, keepdims=True)
        my_named = total(is_me * named)
        my_rank = total(is_me * rank)
        my_weight = total(jnp.where(first == me, weight, 0.0))
        has_backup = total(jnp.where(backup == me, 1.0, 0.0))
        its_first = total(jnp.where(backup == me, first, 0.0))
        its_weight = total(jnp.where(backup == me, weight, 0.0))
        moved = has_backup * total(jnp.where(number == its_first, spilled, 0.0))
        moved_wide = jnp.broadcast_to(moved, (16, 512))
        spill_rank = jnp.dot(moved_wide.astype(bf16), near[...], preferred_element_type=f32)[0:1]
        token = lax.broadcasted_iota(jnp.int32, (1, 512), 1)
        block = lax.shift_right_logical(token, 4).astype(f32)
        kept_slot = lax.broadcasted_iota(jnp.int32, (cap, 512), 0).astype(f32)
        spare_slot = lax.broadcasted_iota(jnp.int32, (slots - cap, 512), 0).astype(f32)
        spare_at = jnp.where(spill_rank < quota, block * quota + spill_rank, -1.0)
        kept_grid = jnp.where(my_rank == kept_slot, my_named, 0.0)
        spare_grid = jnp.where(spare_at == spare_slot, moved, 0.0)
        pick[...] = jnp.concatenate([kept_grid, spare_grid], axis=0).astype(bf16)
        mixing = jnp.concatenate([kept_grid * my_weight, spare_grid * its_weight], axis=0)
        comb[...] = mixing.T.astype(bf16).reshape(16, 2, 16, slots)

    def meta_step(i):
        waits, sends = ((range(0, 3), range(3, 6)), (range(3, 6), range(6, 7)), (range(6, 7), ()))[i]
        for at in waits:
            metas_out[at].wait_recv()
        for at in sends:
            begin(metas_out[at])
        if i == 2:
            route()

    def gather_step(stage, k, b):
        if b in late[k] or stage == 0:
            gathers[k][3, b].wait_recv()
        else:
            for flip in range(2):
                gathers[k][stage - 1, b, flip].wait_recv()
        if stage < 2:
            for flip in range(2):
                begin(gathers[k][stage, b, flip])
            return
        if b == 0:
            for other in late[k]:
                begin(gathers[k][3, other])
        begin(gathers[k][2, b])

    projected = []

    def project(k):
        for b in range(4):
            gathers[k][2, b].wait_recv()
        for copy in weight_copies[k]:
            copy.wait()
        rows = jnp.dot(pick[...], toks[k][...].reshape(512, 2 * halves[k]), preferred_element_type=f32).astype(bf16)
        new_gate = jnp.dot(rows, wg[columns[k], :], preferred_element_type=f32)
        new_up = jnp.dot(rows, wu[columns[k], :], preferred_element_type=f32)
        projected.append(k)
        if len(projected) == 1:
            gate[...] = new_gate
            upward[...] = new_up
        elif len(projected) < count:
            gate[...] += new_gate
            upward[...] += new_up
        else:
            full = gate[...] + new_gate
            hidden[...] = (full / (1.0 + jnp.exp(-full)) * (upward[...] + new_up)).astype(bf16)

    def scatter_copies(k):
        table = {}
        sem = lambda at: (rs_send.at[k, at], rs_recv.at[k, at])
        for b, there in enumerate(planes):
            for flip in range(2):
                one, two = (x_peer, y_peer) if flip else (y_peer, x_peer)
                if b not in late[k]:
                    table[0, b, flip] = remote(to_one[k].at[flip, there], from_one[k].at[flip, there],
                                               *sem(5 * b + flip), one)
                    table[1, b, flip] = remote(to_two[k].at[flip, there], from_two[k].at[flip, there],
                                               *sem(5 * b + 2 + flip), two)
            if b in late[k]:
                at = late[k].index(b)
                table[2, b] = remote(to_plane[k].at[at], from_plane[k].at[at], *sem(5 * b + 4), z_peers[b - 1])
            elif b:
                table[2, b] = remote(to_z[k].at[b - 1], from_z[k].at[b - 1], *sem(5 * b + 4), z_peers[b - 1])
        return table

    cores = [remote(to_core[k], from_core[k], rs_send.at[k, 4], rs_recv.at[k, 4], core_peer) for k in range(count)]
    scatters = [scatter_copies(k) for k in range(count)]

    def produce(k):
        down_copies[k].wait()
        rows = jnp.dot(hidden[...], wd[k][...], preferred_element_type=f32).astype(bf16)
        sides = jnp.concatenate([comb[:, 1 - c].reshape(256, slots), comb[:, c].reshape(256, slots)], axis=0)
        mixed = jnp.dot(sides, rows, preferred_element_type=f32)
        to_core[k][...] = mixed[:256].astype(bf16).reshape(4, 2, 2, 16, 2 * halves[k])
        begin(cores[k])
        own[k][...] = mixed[256:].reshape(4, 2, 2, 16, 2 * halves[k])

    def at_one(k, flip, b, first, second):
        yy, xx = (second, first) if flip else (first, second)
        mine = own[k][planes[b], yy, xx, :, side[k][flip]]
        if late[k] and b == 0:
            return mine
        return mine + from_core[k][planes[b], yy, xx, :, side[k][flip]].astype(f32)

    def at_two(k, flip, b, first, second):
        return at_one(k, flip, b, first, second) + from_one[k][flip, planes[b], second].astype(f32)

    def at_z(k, flip, b):
        first, second = (x, y) if flip else (y, x)
        return at_two(k, flip, b, first, second) + from_two[k][flip, planes[b]].astype(f32)

    joined = []

    def scatter_step(stage, k, b):
        there = planes[b]
        if k not in joined:
            joined.append(k)
            cores[k].wait_recv()
        if stage == 3:
            for at, other in reversed(list(enumerate(late[k]))):
                total = own[k][planes[other]] + from_core[k][planes[other]].astype(f32)
                to_plane[k][at] = total.astype(bf16)
                begin(scatters[k][2, other])
            return
        if stage == 0 and late[k] and b == 0:
            total = own[k][z] + from_core[k][z].astype(f32)
            for at, other in enumerate(late[k]):
                scatters[k][2, other].wait_recv()
                total += from_plane[k][at].astype(f32)
            own[k][z] = total
        for flip in range(2):
            first, second = (x, y) if flip else (y, x)
            if stage == 0:
                for other in range(2):
                    to_one[k][flip, there, other] = at_one(k, flip, b, 1 - first, other).astype(bf16)
            elif stage == 1:
                scatters[k][0, b, flip].wait_recv()
                to_two[k][flip, there] = at_two(k, flip, b, first, 1 - second).astype(bf16)
            else:
                scatters[k][1, b, flip].wait_recv()
                to_z[k][b - 1, :, side[k][flip]] = at_z(k, flip, b).astype(bf16)
            if stage < 2:
                begin(scatters[k][stage, b, flip])
        if stage == 2:
            begin(scatters[k][2, b])

    def finish(k):
        early = [b for b in range(1, 4) if b not in late[k]]
        for b in early:
            scatters[k][2, b].wait_recv()
        for flip in range(2):
            scatters[k][1, 0, flip].wait_recv()
            total = at_z(k, flip, 0)
            for b in early:
                total += from_z[k][b - 1, :, side[k][flip]].astype(f32)
            start = starts[k] + flip * halves[k]
            out_ref[:, start:start + halves[k]] = total.astype(bf16)

    for copy in metas_out[0:3]:
        begin(copy)
    for stage, k, at in first_sends:
        begin(gathers[k][3, at] if stage else gathers[k][0, 0, at])
    weight_copies = []
    for k in range(count):
        pair = [pltpu.make_async_copy(gate_hbm.at[0, columns[k]], wg.at[columns[k]], w_sem.at[0, k]),
                pltpu.make_async_copy(up_hbm.at[0, columns[k]], wu.at[columns[k]], w_sem.at[1, k])]
        weight_copies.append(pair)
        for copy in pair:
            copy.start()
    down_copies = []
    for k in range(count):
        copy = pltpu.make_async_copy(down_hbm.at[0, :, columns[k]], wd[k], w_sem.at[2, k])
        copy.start()
        down_copies.append(copy)

    row = lax.broadcasted_iota(jnp.int32, (512, 512), 0)
    col = lax.broadcasted_iota(jnp.int32, (512, 512), 1)
    before[...] = jnp.where(row < col, 1.0, 0.0).astype(bf16)
    same = lax.shift_right_logical(row, 4) == lax.shift_right_logical(col, 4)
    near[...] = jnp.where(same & (row < col), 1.0, 0.0).astype(bf16)
    for event in order:
        kind, at = event[0], event[1:]
        if kind == SCATTER:
            for copy in started[:DRAINED]:
                copy.wait_send()
            del started[:DRAINED]
        if kind == META:
            meta_step(*at)
        elif kind == GATHER:
            gather_step(*at)
        elif kind == PROJECT:
            project(*at)
        elif kind == PRODUCE:
            produce(*at)
        elif kind == SCATTER:
            scatter_step(*at)
        else:
            finish(*at)

    for copy in started:
        copy.wait_send()


def fused_body(chunks, first_sends, order, tokens, expert_ids, backup_ids, scores, gate_weight, up_weight, down_weight):
    device_count = lax.axis_size(("gx", "gy"))
    tok_rows, top = expert_ids.shape
    model, ff = gate_weight.shape[1:]
    cap = tok_rows * top
    quota = max(1, cap // (4 * device_count))
    slots = cap + device_count * quota
    count = len(chunks)
    bf16, f32 = jnp.bfloat16, jnp.float32
    grid = (4, 2, 2)
    vmem = lambda shape, kind: pltpu.VMEM(shape, kind)
    pairs = lambda lead, kind: tuple(vmem(lead + (tok_rows, 2 * half), kind) for half, _ in chunks)
    each = lambda lead, kind: tuple(vmem((2,) + lead + (tok_rows, half), kind) for half, _ in chunks)
    lines = pairs((3,), bf16)
    to_planes = tuple(vmem((max(1, len(late)), 2, 2, tok_rows, 2 * half), bf16) for half, late in chunks)
    scratch = [
        vmem((top, tok_rows), jnp.int32), vmem((top, tok_rows), jnp.int32), vmem((top, tok_rows), f32),
        pltpu.SemaphoreType.DMA((3 + count,)),
        vmem((128, 128), f32), vmem((512, 512), bf16), vmem((512, 512), bf16), vmem(grid + (2, tok_rows, 128), bf16),
        pairs(grid + (2,), bf16),
        vmem((model, ff), bf16), vmem((model, ff), bf16), tuple(vmem((ff, 2 * half), bf16) for half, _ in chunks),
        vmem((slots, 512), bf16), vmem((16, 2, tok_rows, slots), bf16),
        vmem((slots, ff), f32), vmem((slots, ff), f32), vmem((slots, ff), bf16),
        pairs(grid, f32), pairs(grid, bf16), pairs(grid, bf16),
        each((4, 2), bf16), each((4, 2), bf16), each((4,), bf16), each((4,), bf16), lines, lines, to_planes, to_planes,
        pltpu.SemaphoreType.DMA((7,)), pltpu.SemaphoreType.DMA((7,)),
        pltpu.SemaphoreType.DMA((count, 24)), pltpu.SemaphoreType.DMA((count, 24)),
        pltpu.SemaphoreType.DMA((count, 20)), pltpu.SemaphoreType.DMA((count, 20)),
        pltpu.SemaphoreType.DMA((3, count)),
    ]
    whole = pl.BlockSpec(memory_space=pltpu.VMEM)
    away = pl.BlockSpec(memory_space=pl.ANY)
    return pl.pallas_call(
        functools.partial(exchange, (chunks, first_sends, order, device_count, cap, quota, slots, top)),
        out_shape=pltpu.VMEM((tok_rows, model), bf16),
        in_specs=[away] * 7,
        out_specs=whole,
        scratch_shapes=scratch,
        compiler_params=pltpu.CompilerParams(
            collective_id=0, has_side_effects=True, vmem_limit_bytes=60 * 1024 * 1024),
    )(tokens, expert_ids.T, backup_ids.T, scores.T, gate_weight, up_weight, down_weight)


DRAINED = 4
META, GATHER, PROJECT, PRODUCE, SCATTER, FINISH = range(6)
CHUNKS = ((896, ()), (640, ()), (256, (1, 2, 3)))
FIRST = (
    (3, 0, 3), (0, 0, 0), (3, 0, 1), (0, 0, 1), (0, 2, 1), (3, 0, 2), (0, 2, 0), (3, 1, 1), (3, 1, 2),
    (0, 1, 0), (0, 1, 1), (3, 1, 3),
)
ORDER = (
    (GATHER, 1, 0, 0), (GATHER, 1, 2, 0), (META, 0), (GATHER, 0, 0, 1), (GATHER, 1, 1, 0), (GATHER, 0, 0, 2),
    (GATHER, 0, 0, 3), (GATHER, 0, 1, 1), (GATHER, 2, 2, 0), (GATHER, 1, 0, 1), (GATHER, 1, 0, 2),
    (GATHER, 0, 1, 2), (GATHER, 1, 0, 3), (GATHER, 0, 1, 3), (META, 1), (GATHER, 1, 1, 1), (GATHER, 2, 2, 1),
    (META, 2), (GATHER, 2, 0, 0), (GATHER, 1, 1, 2), (GATHER, 2, 1, 0), (GATHER, 2, 0, 2), (GATHER, 2, 0, 1),
    (GATHER, 2, 2, 2), (GATHER, 2, 0, 3), (GATHER, 1, 1, 3), (GATHER, 2, 2, 3), (GATHER, 2, 1, 1), (PROJECT, 0),
    (GATHER, 2, 1, 2), (GATHER, 2, 1, 3), (PROJECT, 2), (PROJECT, 1), (PRODUCE, 0), (PRODUCE, 1),
    (SCATTER, 0, 0, 3), (PRODUCE, 2), (SCATTER, 0, 0, 1), (SCATTER, 0, 0, 2), (SCATTER, 0, 1, 2),
    (SCATTER, 3, 2, 0), (SCATTER, 1, 0, 3), (SCATTER, 0, 1, 3), (SCATTER, 1, 0, 2), (SCATTER, 0, 1, 1),
    (SCATTER, 1, 0, 1), (SCATTER, 1, 1, 2), (SCATTER, 2, 0, 3), (SCATTER, 1, 1, 3), (SCATTER, 1, 1, 1),
    (SCATTER, 0, 1, 0), (SCATTER, 2, 0, 2), (SCATTER, 0, 0, 0), (SCATTER, 2, 0, 1), (SCATTER, 0, 2, 0),
    (SCATTER, 2, 1, 3), (SCATTER, 2, 1, 1), (SCATTER, 1, 1, 0), (SCATTER, 2, 1, 2), (SCATTER, 1, 0, 0),
    (SCATTER, 1, 2, 0), (FINISH, 0), (FINISH, 2), (FINISH, 1),
)


def pick_body(mesh):
    if mesh.shape["gx"] == 4 and mesh.shape["gy"] == 8:
        return functools.partial(fused_body, CHUNKS, FIRST, ORDER)
    return on_device


def solution(mesh):
    placed = (
        P(("gx", "gy"), None),
        P(("gx", "gy"), None),
        P(("gx", "gy"), None),
        P(("gx", "gy"), None),
        P(("gx", "gy"), None, None),
        P(("gx", "gy"), None, None),
        P(("gx", "gy"), None, None),
    )
    return jax.shard_map(
        pick_body(mesh), mesh=mesh, in_specs=placed, out_specs=P(("gx", "gy"), None), check_vma=False
    )
```
